256 devices in a mesh: grp: 8 (over y, core), dev: 32 (over z, x).
Axes of the slice: x: 4, y: 4, z: 8, core: 2. Of those that a mesh axis runs over, the one named last changes fastest.
Arguments:
- blocks: bfloat16 [8, 32, 12, 64, 1728], P('grp', 'dev'), may hold values from -0.75 to 0.75
- prolong: bfloat16 [8, 32, 12, 64, 256], P('grp', 'dev'), may hold values from -0.75 to 0.75
- block_cols: int32 [8, 32, 12, 27], P('grp', 'dev'), may hold values from -1 to 95, as said below
- fetch_rows: int32 [8, 32, 32, 3], P('grp', 'dev'), may hold values from 0 to 11
- tile_slot: int32 [8, 32, 12, 27], P('grp', 'dev'), may hold values from 0 to 15
- tile_owner: int32 [8, 32, 16], P('grp', 'dev'), may hold values from 0 to 255, as said below
- tile_place: int32 [8, 32, 16], P('grp', 'dev'), may hold values from 0 to 1
Outputs:
- coarse: float32 [8, 32, 2, 256, 256], P('grp', 'dev')
The draws below stay inside these ranges and needn't reach their ends.
Inputs may be any that keep to these rules, and one draw needn't show every extreme that they name: `block_cols`: -1 marks a padded block slot; at most 243 slots of one device are not padding, exactly 243 on the first device. `tile_owner`: the 16 tiles of one device go to owners of distinct dev indices; at most 4 of them go to owners in one group, exactly 4 to the device's own group.
All inputs are finite; a program needn't handle non-finite values.
Results may differ from the reference program's by a relative error of at most 0.004.
Values may be sent and summed in bfloat16 or wider, within the bound.
No kernel may reach another device: no remote copies, remote signals or barrier semaphores. Data moves between devices by JAX's collectives and lax.ppermute only.
A program may use at most 128 MiB of HBM per device.

```python
import jax
import jax.numpy as jnp
from jax import lax

BLOCK = 64
W = 256
R = 12
K = 27
CT = 2
NCAP = 3
LIVE = 243
LT = 16
N_GRP = 8
N_DEV = 32


def draw_block_cols(key, part):

    def one_device(device_key, first_flag):
        key_count, key_rank, key_cols = jax.random.split(device_key, 3)
        live_count = LIVE - jax.random.randint(key_count, (), 0, LIVE // 2 + 1)
        live_count = jnp.where(first_flag, LIVE, live_count)
        ranking = jax.random.permutation(key_rank, R * K)
        column_ids = jax.random.randint(key_cols, (R * K,), 0, N_DEV * NCAP)
        return jnp.where(ranking < live_count, column_ids, -1).reshape(R, K)
    device_keys = jax.random.split(jax.random.fold_in(key, 11), N_GRP * N_DEV)
    first_flags = jnp.arange(N_GRP * N_DEV) == 0
    result = jax.vmap(one_device)(device_keys, first_flags)
    return result.reshape(N_GRP, N_DEV, R, K).astype(jnp.int32)


def draw_tile_owner(key, part):

    def one_device(device_key, group_id):
        key_devs, key_offsets = jax.random.split(device_key, 2)
        dev_ids = jax.random.permutation(key_devs, N_DEV)[:LT]
        position = jnp.arange(LT)
        offsets = jnp.where(position < LT // 4, 0, 1 + (position - LT // 4) % (N_GRP - 1))
        offsets = jax.random.permutation(key_offsets, offsets)
        return (group_id + offsets) % N_GRP * N_DEV + dev_ids
    device_keys = jax.random.split(jax.random.fold_in(key, 23), N_GRP * N_DEV)
    group_ids = jnp.repeat(jnp.arange(N_GRP), N_DEV)
    result = jax.vmap(one_device)(device_keys, group_ids)
    return result.reshape(N_GRP, N_DEV, LT).astype(jnp.int32)


def plant(values, key, smallest, high):
    extent = values.shape
    index_at = [jax.random.randint(jax.random.fold_in(key, axis), (), 0, extent[axis]) for axis in range(len(extent))]
    values = values.at[tuple(index_at)].set(smallest)
    longest = extent.index(max(extent))
    index_at[longest] = (index_at[longest] + 1) % extent[longest]
    return values.at[tuple(index_at)].set(high)


def block_levels(stream_key, extent, pieces, smallest, high):
    def one(axis_at, shards_of):
        steps = jax.random.uniform(jax.random.fold_in(jax.random.fold_in(stream_key, 6), axis_at), (shards_of,), jnp.float32, smallest / len(pieces), high / len(pieces))
        return jnp.repeat(jnp.exp(steps), extent[axis_at] // shards_of).reshape((-1,) + (1,) * (len(extent) - axis_at - 1))

    level = one(*pieces[0])
    for cut in pieces[1:]:
        level = level * one(*cut)
    return level


def noise(rng, extent, scale, reach, cuts=(), kind=jnp.bfloat16):
    values = scale * jax.random.normal(rng, extent, jnp.float32)
    if cuts:
        values = values * block_levels(rng, extent, cuts, -0.22, 0.18)
    return jnp.clip(values, -reach, reach).astype(kind)


def setup_inputs(seed: int = 0) -> dict:
    streams_of = jax.random.split(jax.random.key(seed), 8)
    return {
        "blocks": noise(streams_of[0], (N_GRP, N_DEV, R, BLOCK, K * BLOCK), BLOCK ** -0.5, 0.75, ((0, 8), (1, 32))),
        "prolong": noise(streams_of[1], (N_GRP, N_DEV, R, BLOCK, W), BLOCK ** -0.5, 0.75, ((0, 8), (1, 32))),
        "block_cols": draw_block_cols(jax.random.fold_in(streams_of[7], 71), 0),
        "fetch_rows": plant(jax.random.randint(streams_of[3], (N_GRP, N_DEV, N_DEV, NCAP), 0, R), jax.random.fold_in(streams_of[3], 1), 0, R - 1).astype(jnp.int32),
        "tile_slot": plant(jax.random.randint(streams_of[4], (N_GRP, N_DEV, R, K), 0, LT), jax.random.fold_in(streams_of[4], 1), 0, LT - 1).astype(jnp.int32),
        "tile_owner": draw_tile_owner(jax.random.fold_in(streams_of[7], 71), 0),
        "tile_place": plant(jax.random.randint(streams_of[6], (N_GRP, N_DEV, LT), 0, CT), jax.random.fold_in(streams_of[6], 1), 0, CT - 1).astype(jnp.int32),
    }


def device_tiles(row_blocks, row_panels, row_columns, row_slots, arrived):
    def one_row(running, item):
        block_row, panel_row, column_ids, slot_ids = item
        matrix = block_row.reshape(BLOCK, K, BLOCK).astype(jnp.float32)
        near_panels = arrived[jnp.maximum(column_ids, 0)].astype(jnp.float32)
        product = jnp.einsum("rkc,kcw->krw", matrix, near_panels)
        product = jnp.where((column_ids >= 0)[:, None, None], product, 0.0).astype(jnp.bfloat16)
        outer_tile = jnp.einsum("ra,krb->kab", panel_row.astype(jnp.float32), product.astype(jnp.float32))
        return running.at[slot_ids].add(outer_tile), None

    running = jnp.zeros((LT, W, W), jnp.float32)
    running, unused = lax.scan(one_row, running, (row_blocks, row_panels, row_columns, row_slots))
    return running.astype(jnp.bfloat16)


def reference(blocks, prolong, block_cols, fetch_rows, tile_slot, tile_owner, tile_place):
    coarse_sum = jnp.zeros((N_GRP * N_DEV * CT, W, W), jnp.float32)

    def per_device(running, flat_index):
        group_id = flat_index // N_DEV
        device_id = flat_index % N_DEV
        chosen = fetch_rows[group_id][:, device_id, :]
        group_panels = prolong[group_id]
        arrived = group_panels[jnp.arange(N_DEV, dtype=jnp.int32)[:, None], chosen]
        arrived = arrived.reshape(N_DEV * NCAP, BLOCK, W)
        partial_value = device_tiles(blocks[group_id, device_id], group_panels[device_id],
                               block_cols[group_id, device_id], tile_slot[group_id, device_id], arrived)
        target_ids = tile_owner[group_id, device_id] * CT + tile_place[group_id, device_id]
        return running.at[target_ids].add(partial_value.astype(jnp.float32)), None

    coarse_sum, unused = lax.scan(per_device, coarse_sum, jnp.arange(N_GRP * N_DEV, dtype=jnp.int32))
    return coarse_sum.reshape(N_GRP, N_DEV, CT, W, W)
```

```python
import functools

import jax
import jax.numpy as jnp
from jax import lax
from jax.experimental import pallas as pl
from jax.experimental.pallas import tpu as pltpu
from jax.sharding import PartitionSpec as P

BLOCK = 64
W = 256
R = 12
K = 27
CT = 2
NCAP = 3
LT = 16
PAIR = 2 * BLOCK


def tiles_kernel(cols_ref, slots_ref, places_ref, a_ref, pt_ref, b_ref, out_ref, near_ref):
    row = pl.program_id(0)
    width = b_ref.shape[-1]
    rows_of = pl.ds(row * BLOCK, BLOCK)

    @pl.when(row == 0)
    def _():
        @pl.loop(0, LT)
        def _(t):
            near_ref[t] = jnp.zeros(near_ref.shape[1:], jnp.float32)

    lane = lax.broadcasted_iota(jnp.int32, (BLOCK, PAIR), 1)
    left = jnp.where(lane < BLOCK, 1.0, 0.0).astype(jnp.bfloat16)
    right = jnp.where(lane < BLOCK, 0.0, 1.0).astype(jnp.bfloat16)

    def target(k):
        return jnp.where(cols_ref[row, k] < 0, LT, slots_ref[row, k])

    def panel(k):
        return b_ref[jnp.maximum(cols_ref[row, k], 0)]

    def add(k, product):
        rounded = product.astype(jnp.bfloat16).astype(jnp.float32)
        near_ref[target(k), rows_of, :] += rounded

    for j in range(K // 2):
        pair = a_ref[0, :, j * PAIR : (j + 1) * PAIR]
        both = jnp.concatenate([pair * left, pair * right], axis=0)
        panels = jnp.concatenate([panel(2 * j), panel(2 * j + 1)], axis=0)
        product = jnp.dot(both, panels, preferred_element_type=jnp.float32)
        add(2 * j, product[:BLOCK])
        add(2 * j + 1, product[BLOCK:])
    last = a_ref[0, :, (K - 1) * BLOCK :]
    add(K - 1, jnp.dot(last, panel(K - 1), preferred_element_type=jnp.float32))

    @pl.when(row == R - 1)
    def _():
        @pl.loop(0, LT)
        def _(t):
            near = near_ref[t]
            high = near.astype(jnp.bfloat16)
            low = (near - high.astype(jnp.float32)).astype(jnp.bfloat16)
            tile = jnp.dot(pt_ref[...], high, preferred_element_type=jnp.float32)
            tile += jnp.dot(pt_ref[...], low, preferred_element_type=jnp.float32)
            out_ref[places_ref[t]] = tile.astype(jnp.bfloat16)


def device_tiles(blocks, pt, arrived, cols, slots, places, n_places):
    width = arrived.shape[-1]
    return pl.pallas_call(
        tiles_kernel,
        out_shape=jax.ShapeDtypeStruct((n_places, W, width), jnp.bfloat16),
        grid_spec=pltpu.PrefetchScalarGridSpec(
            num_scalar_prefetch=3,
            grid=(R,),
            in_specs=[
                pl.BlockSpec((1, BLOCK, K * BLOCK), lambda i, *_: (i, 0, 0)),
                pl.BlockSpec((W, R * BLOCK), lambda i, *_: (0, 0)),
                pl.BlockSpec(arrived.shape, lambda i, *_: (0, 0, 0)),
            ],
            out_specs=pl.BlockSpec((n_places, W, width), lambda i, *_: (0, 0, 0)),
            scratch_shapes=[pltpu.VMEM((LT + 1, R * BLOCK, width), jnp.float32)],
        ),
        compiler_params=pltpu.CompilerParams(
            dimension_semantics=("arbitrary",), vmem_limit_bytes=60 << 20
        ),
        cost_estimate=pl.CostEstimate(
            flops=8_000_000_000 * width // W,
            bytes_accessed=10_000_000 * width // W,
            transcendentals=0,
        ),
        name="device_tiles",
    )(cols, slots, places, blocks, pt, arrived)


def table_kernel(labels_ref, got_ref, table_ref, sum_ref):
    spread = table_ref.shape[0]

    @pl.loop(0, spread)
    def _(t):
        sum_ref[t] = jnp.zeros(sum_ref.shape[1:], jnp.float32)

    @pl.loop(0, got_ref.shape[0])
    def _(s):
        label = labels_ref[s]
        at = jnp.where(label < 0, spread, label)
        sum_ref[at] += got_ref[s].astype(jnp.float32)

    @pl.loop(0, spread)
    def _(t):
        table_ref[t] = sum_ref[t].astype(table_ref.dtype)


def table_of(labels, got, spread):
    n, _, width = got.shape
    rows = 64
    return pl.pallas_call(
        table_kernel,
        out_shape=jax.ShapeDtypeStruct((spread, W, width), jnp.bfloat16),
        grid_spec=pltpu.PrefetchScalarGridSpec(
            num_scalar_prefetch=1,
            grid=(W // rows,),
            in_specs=[pl.BlockSpec((n, rows, width), lambda i, *_: (0, i, 0))],
            out_specs=pl.BlockSpec((spread, rows, width), lambda i, *_: (0, i, 0)),
            scratch_shapes=[pltpu.VMEM((spread + 1, rows, width), jnp.float32)],
        ),
        compiler_params=pltpu.CompilerParams(dimension_semantics=("arbitrary",)),
        cost_estimate=pl.CostEstimate(
            flops=n * W * width, bytes_accessed=6_000_000 * width // W, transcendentals=0
        ),
        name="table_of",
    )(labels, got)


def body(blocks, prolong, block_cols, fetch_rows, tile_slot, tile_owner, tile_place):
    dev_count = lax.axis_size("dev")
    grp_count = lax.axis_size("grp")
    panels = prolong[0, 0]
    outgoing = panels[fetch_rows[0, 0]].reshape(dev_count, NCAP * BLOCK, W)
    arrived = lax.all_to_all(outgoing, "dev", split_axis=0, concat_axis=0, tiled=True)
    arrived = arrived.reshape(dev_count * NCAP, BLOCK, W)

    owners = tile_owner[0, 0]
    dev_target = owners % dev_count
    label = (owners // dev_count) * CT + tile_place[0, 0]
    labels = jnp.full((dev_count,), -1, jnp.int32).at[dev_target].set(label)
    got_labels = lax.all_to_all(labels, "dev", split_axis=0, concat_axis=0, tiled=True)

    pt = panels.reshape(R * BLOCK, W).T
    sending = device_tiles(
        blocks[0, 0], pt, arrived, block_cols[0, 0], tile_slot[0, 0], dev_target, dev_count
    )
    got = lax.all_to_all(sending, "dev", split_axis=0, concat_axis=0, tiled=True)
    table = table_of(got_labels, got, grp_count * CT)
    parts = lax.all_to_all(table, "grp", split_axis=0, concat_axis=0, tiled=True)
    parts = parts.reshape(grp_count, CT, W, W).astype(jnp.float32)
    return parts.sum(0).reshape(1, 1, CT, W, W)


def solution(mesh):
    return jax.shard_map(
        body,
        mesh=mesh,
        in_specs=(
            P("grp", "dev", None, None, None),
            P("grp", "dev", None, None, None),
            P("grp", "dev", None, None),
            P("grp", "dev", None, None),
            P("grp", "dev", None, None),
            P("grp", "dev", None),
            P("grp", "dev", None),
        ),
        out_specs=P("grp", "dev", None, None, None),
        check_vma=False,
    )
```

```python
import functools

import jax
import jax.numpy as jnp
from jax import lax
from jax.experimental import pallas as pl
from jax.experimental.pallas import tpu as pltpu
from jax.sharding import PartitionSpec as P


BLOCK = 64
W = 256
R = 12
K = 27
CT = 2
NCAP = 3
LT = 16
PAIR = 2 * BLOCK
HALVES = 1
STEPS = (1, -1, 2)


def pick_kernel(n_x, ups, asks_ref, *refs):
    block_refs, out_refs = refs[: len(ups)], refs[len(ups) :]
    z, x = lax.axis_index("dev") // n_x, lax.axis_index("dev") % n_x
    n_z = asks_ref.shape[0] // n_x
    for i, (up, block_ref) in enumerate(zip(ups, block_refs)):
        source = (z + n_z - up) % n_z * n_x + x
        for step, out_ref in zip(STEPS, out_refs):
            peer = (x + n_x + step) % n_x
            for c in range(NCAP):
                out_ref[i * NCAP + c] = block_ref[asks_ref[source, 1 + peer * NCAP + c]]


def pick(asks, n_x, ups, blocks):
    shape = (len(blocks) * NCAP,) + blocks[0].shape[1:]
    whole = lambda shape: pl.BlockSpec(shape, lambda i, *_: (0,) * len(shape))
    return pl.pallas_call(
        functools.partial(pick_kernel, n_x, ups),
        out_shape=[jax.ShapeDtypeStruct(shape, blocks[0].dtype)] * len(STEPS),
        grid_spec=pltpu.PrefetchScalarGridSpec(
            num_scalar_prefetch=1,
            grid=(1,),
            in_specs=[whole(b.shape) for b in blocks],
            out_specs=[whole(shape)] * len(STEPS),
        ),
        cost_estimate=pl.CostEstimate(flops=0, bytes_accessed=1_500_000, transcendentals=0),
        name="pick",
    )(asks, *blocks)


def fetch(panels, rows_of, labels):
    n_z, n_x = 8, 4
    half = n_z // 2
    me = lax.axis_index("dev")
    z, x = me // n_x, me % n_x

    def along_z(step):
        return [(s, (s // n_x + step) % n_z * n_x + s % n_x) for s in range(n_z * n_x)]

    def along_x(step):
        return [(s, s // n_x * n_x + (s % n_x + step) % n_x) for s in range(n_z * n_x)]

    def forward(asks, ups, blocks):
        picked = pick(asks, n_x, ups, blocks)
        return [lax.ppermute(p, "dev", along_x(step)) for p, step in zip(picked, STEPS)]

    fetched = rows_of.reshape(n_z, 1, n_x * NCAP)
    first = jnp.broadcast_to(fetched, (n_z, n_x, n_x * NCAP)).reshape(n_z * n_x, n_x * NCAP)
    asked = jnp.concatenate([labels[:, None], first], axis=1)

    up = lax.ppermute(panels, "dev", along_z(1))
    down = lax.ppermute(panels, "dev", along_z(-1))
    asks = lax.all_to_all(asked, "dev", split_axis=0, concat_axis=0, tiled=True)
    blocks = {0: panels}
    sent = {0: forward(asked, (0,), (panels,))}
    for k in range(1, half):
        blocks[n_z - k], blocks[k] = up, down
        if k + 1 < half:
            new_up = lax.ppermute(up, "dev", along_z(1))
            new_down = lax.ppermute(down, "dev", along_z(-1))
        else:
            odd = lax.axis_index("grp") % 2 == 1
            n = n_z * n_x
            pairs = [
                (g * n + s, g * n + t)
                for g in range(lax.axis_size("grp"))
                for s, t in along_z(-1 if g % 2 else 1)
            ]
            far = lax.ppermute(jnp.where(odd, down, up), ("grp", "dev"), pairs)
        sent[k] = forward(asks, (k, -k), (up, down))
        up, down = new_up, new_down
    blocks[half] = far
    sent[half] = forward(asks, (half,), (far,))

    entry = jnp.arange(n_z * n_x * NCAP, dtype=jnp.int32)
    s, c = entry // NCAP, entry % NCAP
    dz, dx = (s // n_x - z) % n_z, (s % n_x - x) % n_x
    table = asks[:, 1:].reshape(n_z, n_x, n_x, NCAP)
    column = jnp.arange(n_x)[:, None] == x
    own = jnp.sum(jnp.where(column[None, :, :, None] & column.T[None, :, :, None], table, 0), (1, 2))
    own = jnp.broadcast_to(own[:, None, :], (n_z, n_x, NCAP)).reshape(-1)
    there = n_z * R + (dx - 1) * (n_z * NCAP) + dz * NCAP + c
    where = jnp.where(dx == 0, dz * R + own, there).astype(jnp.int32)

    pieces, spots = [], []
    for d in range(n_z):
        pieces.append(blocks[d])
        spots.append([(0, R, d * R)])
    for j, step in enumerate(STEPS):
        base = n_z * R + ((-step) % n_x - 1) * (n_z * NCAP)
        for k in range(half + 1):
            pieces.append(sent[k][j])
            if k in (0, half):
                spots.append([(0, NCAP, base + k * NCAP)])
            else:
                spots.append([(0, NCAP, base + (n_z - k) * NCAP), (NCAP, NCAP, base + k * NCAP)])
    return pieces, spots, where, asks[:, 0]


def tiles_kernel(spots, first, cols_ref, slots_ref, places_ref, where_ref, a_ref, pt_ref, *refs):
    piece_refs, (out_ref, b_ref, near_ref, sems) = refs[: len(spots)], refs[len(spots) :]
    row = pl.program_id(0)
    width = b_ref.shape[-1]
    rows_of = pl.ds(row * BLOCK, BLOCK)

    @pl.when(row == 0)
    def _():
        copies = []
        for piece_ref, parts in zip(piece_refs, spots):
            for start, n, place in parts:
                copies.append(
                    pltpu.make_async_copy(
                        piece_ref.at[pl.ds(start, n), :, pl.ds(first, width)],
                        b_ref.at[pl.ds(place, n)],
                        sems.at[len(copies)],
                    )
                )
                copies[-1].start()

        @pl.loop(0, LT)
        def _(t):
            near_ref[t] = jnp.zeros(near_ref.shape[1:], jnp.float32)

        for copy in copies:
            copy.wait()

    lane = lax.broadcasted_iota(jnp.int32, (BLOCK, PAIR), 1)
    left = jnp.where(lane < BLOCK, 1.0, 0.0).astype(jnp.bfloat16)
    right = jnp.where(lane < BLOCK, 0.0, 1.0).astype(jnp.bfloat16)

    def target(k):
        return jnp.where(cols_ref[row, k] < 0, LT, slots_ref[row, k])

    def panel(k):
        return b_ref[where_ref[jnp.maximum(cols_ref[row, k], 0)]]

    def add(k, product):
        rounded = product.astype(jnp.bfloat16).astype(jnp.float32)
        near_ref[target(k), rows_of, :] += rounded

    for j in range(K // 2):
        pair = a_ref[0, :, j * PAIR : (j + 1) * PAIR]
        both = jnp.concatenate([pair * left, pair * right], axis=0)
        panels = jnp.concatenate([panel(2 * j), panel(2 * j + 1)], axis=0)
        product = jnp.dot(both, panels, preferred_element_type=jnp.float32)
        add(2 * j, product[:BLOCK])
        add(2 * j + 1, product[BLOCK:])
    last = a_ref[0, :, (K - 1) * BLOCK :]
    add(K - 1, jnp.dot(last, panel(K - 1), preferred_element_type=jnp.float32))

    @pl.when(row == R - 1)
    def _():
        @pl.loop(0, LT)
        def _(t):
            near = near_ref[t]
            high = near.astype(jnp.bfloat16)
            low = (near - high.astype(jnp.float32)).astype(jnp.bfloat16)
            tile = jnp.dot(pt_ref[...], high, preferred_element_type=jnp.float32)
            tile += jnp.dot(pt_ref[...], low, preferred_element_type=jnp.float32)
            out_ref[places_ref[t]] = tile.astype(jnp.bfloat16)


def device_tiles(blocks, pt, pieces, spots, where, cols, slots, places, n_places, first, width):
    n_copies = sum(len(parts) for parts in spots)
    n_panels = max(place + n for parts in spots for _, n, place in parts)
    return pl.pallas_call(
        functools.partial(tiles_kernel, spots, first),
        out_shape=jax.ShapeDtypeStruct((n_places, W, width), jnp.bfloat16),
        grid_spec=pltpu.PrefetchScalarGridSpec(
            num_scalar_prefetch=4,
            grid=(R,),
            in_specs=[
                pl.BlockSpec((1, BLOCK, K * BLOCK), lambda i, *_: (i, 0, 0)),
                pl.BlockSpec((W, R * BLOCK), lambda i, *_: (0, 0)),
            ]
            + [pl.BlockSpec(memory_space=pltpu.HBM)] * len(pieces),
            out_specs=pl.BlockSpec((n_places, W, width), lambda i, *_: (0, 0, 0)),
            scratch_shapes=[
                pltpu.VMEM((n_panels, BLOCK, width), jnp.bfloat16),
                pltpu.VMEM((LT + 1, R * BLOCK, width), jnp.float32),
                pltpu.SemaphoreType.DMA((n_copies,)),
            ],
        ),
        compiler_params=pltpu.CompilerParams(
            dimension_semantics=("arbitrary",), vmem_limit_bytes=60 << 20
        ),
        cost_estimate=pl.CostEstimate(
            flops=8_000_000_000 * width // W,
            bytes_accessed=20_000_000 * width // W,
            transcendentals=0,
        ),
        name="device_tiles",
    )(cols, slots, places, where, blocks, pt, *pieces)


def table_kernel(labels_ref, got_ref, table_ref, sum_ref):
    spread = table_ref.shape[0]

    @pl.loop(0, spread)
    def _(t):
        sum_ref[t] = jnp.zeros(sum_ref.shape[1:], jnp.float32)

    @pl.loop(0, got_ref.shape[0])
    def _(s):
        label = labels_ref[s]
        at = jnp.where(label < 0, spread, label)
        sum_ref[at] += got_ref[s].astype(jnp.float32)

    @pl.loop(0, spread)
    def _(t):
        table_ref[t] = sum_ref[t].astype(table_ref.dtype)


def table_of(labels, got, spread):
    n, _, width = got.shape
    rows = 64
    return pl.pallas_call(
        table_kernel,
        out_shape=jax.ShapeDtypeStruct((spread, W, width), jnp.bfloat16),
        grid_spec=pltpu.PrefetchScalarGridSpec(
            num_scalar_prefetch=1,
            grid=(W // rows,),
            in_specs=[pl.BlockSpec((n, rows, width), lambda i, *_: (0, i, 0))],
            out_specs=pl.BlockSpec((spread, rows, width), lambda i, *_: (0, i, 0)),
            scratch_shapes=[pltpu.VMEM((spread + 1, rows, width), jnp.float32)],
        ),
        compiler_params=pltpu.CompilerParams(dimension_semantics=("arbitrary",)),
        cost_estimate=pl.CostEstimate(
            flops=n * W * width, bytes_accessed=6_000_000 * width // W, transcendentals=0
        ),
        name="table_of",
    )(labels, got)


def layer(blocks, prolong, block_cols, fetch_rows, tile_slot, tile_owner, tile_place):
    dev_count = lax.axis_size("dev")
    grp_count = lax.axis_size("grp")
    panels = prolong[0, 0]
    owners = tile_owner[0, 0]
    dev_target = owners % dev_count
    label = (owners // dev_count) * CT + tile_place[0, 0]
    meant = dev_target[None, :] == jnp.arange(dev_count)[:, None]
    labels = jnp.max(jnp.where(meant, label[None, :], -1), axis=1)
    pieces, spots, where, got_labels = fetch(panels, fetch_rows[0, 0], labels)

    pt = panels.reshape(R * BLOCK, W).T
    parts = []
    width = W // HALVES
    for h in range(HALVES):
        sending = device_tiles(
            blocks[0, 0], pt, pieces, spots, where, block_cols[0, 0], tile_slot[0, 0],
            dev_target, dev_count, h * width, width,
        )
        got = lax.all_to_all(sending, "dev", split_axis=0, concat_axis=0, tiled=True)
        table = table_of(got_labels, got, grp_count * CT)
        part = lax.all_to_all(table, "grp", split_axis=0, concat_axis=0, tiled=True)
        part = part.reshape(grp_count, CT, W, width).astype(jnp.float32)
        parts.append(part.sum(0))
    return jnp.concatenate(parts, axis=-1).reshape(1, 1, CT, W, W)


def solution(mesh):
    return jax.shard_map(
        layer,
        mesh=mesh,
        in_specs=(
            P("grp", "dev", None, None, None),
            P("grp", "dev", None, None, None),
            P("grp", "dev", None, None),
            P("grp", "dev", None, None),
            P("grp", "dev", None, None),
            P("grp", "dev", None),
            P("grp", "dev", None),
        ),
        out_specs=P("grp", "dev", None, None, None),
        check_vma=False,
    )
```

```python
import functools

import jax
import jax.numpy as jnp
from jax import lax
from jax.experimental import pallas as pl
from jax.experimental.pallas import tpu as pltpu
from jax.sharding import PartitionSpec as P


BLOCK = 64
W = 256
R = 12
K = 27
CT = 2
NCAP = 3
LT = 16
PAIR = 2 * BLOCK
HALVES = 2
STEPS = (1, -1, 2)


def pick_kernel(n_x, ups, asks_ref, *refs):
    block_refs, out_refs = refs[: len(ups)], refs[len(ups) :]
    z, x = lax.axis_index("dev") // n_x, lax.axis_index("dev") % n_x
    n_z = asks_ref.shape[0] // n_x
    for i, (up, block_ref) in enumerate(zip(ups, block_refs)):
        source = (z + n_z - up) % n_z * n_x + x
        for step, out_ref in zip(STEPS, out_refs):
            peer = (x + n_x + step) % n_x
            for c in range(NCAP):
                out_ref[i * NCAP + c] = block_ref[asks_ref[source, 1 + peer * NCAP + c]]


def pick(asks, n_x, ups, blocks):
    shape = (len(blocks) * NCAP,) + blocks[0].shape[1:]
    vmem = pl.BlockSpec(memory_space=pltpu.VMEM)
    return pl.pallas_call(
        functools.partial(pick_kernel, n_x, ups),
        out_shape=[jax.ShapeDtypeStruct(shape, blocks[0].dtype)] * len(STEPS),
        in_specs=[pl.BlockSpec(memory_space=pltpu.SMEM)] + [vmem] * len(blocks),
        out_specs=[vmem] * len(STEPS),
        compiler_params=pltpu.CompilerParams(vmem_limit_bytes=16 << 20),
        cost_estimate=pl.CostEstimate(flops=0, bytes_accessed=1_500_000, transcendentals=0),
        name="pick",
    )(asks, *blocks)


def fetch(panels, rows_of, labels):
    n_z, n_x = 8, 4
    half = n_z // 2
    me = lax.axis_index("dev")
    z, x = me // n_x, me % n_x

    def along_z(step):
        return [(s, (s // n_x + step) % n_z * n_x + s % n_x) for s in range(n_z * n_x)]

    def along_x(step):
        return [(s, s // n_x * n_x + (s % n_x + step) % n_x) for s in range(n_z * n_x)]

    def forward(asks, ups, blocks):
        picked = pick(asks, n_x, ups, blocks)
        return [lax.ppermute(p, "dev", along_x(step)) for p, step in zip(picked, STEPS)]

    fetched = rows_of.reshape(n_z, 1, n_x * NCAP)
    first = jnp.broadcast_to(fetched, (n_z, n_x, n_x * NCAP)).reshape(n_z * n_x, n_x * NCAP)
    asked = jnp.concatenate([labels[:, None], first], axis=1)

    up = lax.ppermute(panels, "dev", along_z(1))
    down = lax.ppermute(panels, "dev", along_z(-1))
    asks = lax.all_to_all(asked, "dev", split_axis=0, concat_axis=0, tiled=True)
    blocks = {0: panels}
    sent = {0: forward(asked, (0,), (panels,))}
    for k in range(1, half):
        blocks[n_z - k], blocks[k] = up, down
        if k + 1 < half:
            new_up = lax.ppermute(up, "dev", along_z(1))
            new_down = lax.ppermute(down, "dev", along_z(-1))
        else:
            odd = lax.axis_index("grp") % 2 == 1
            n = n_z * n_x
            pairs = [
                (g * n + s, g * n + t)
                for g in range(lax.axis_size("grp"))
                for s, t in along_z(-1 if g % 2 else 1)
            ]
            far = lax.ppermute(jnp.where(odd, down, up), ("grp", "dev"), pairs)
        sent[k] = forward(asks, (k, -k), (up, down))
        up, down = new_up, new_down
    blocks[half] = far
    sent[half] = forward(asks, (half,), (far,))

    entry = jnp.arange(n_z * n_x * NCAP, dtype=jnp.int32)
    s, c = entry // NCAP, entry % NCAP
    dz, dx = (s // n_x - z) % n_z, (s % n_x - x) % n_x
    table = asks[:, 1:].reshape(n_z, n_x, n_x, NCAP)
    column = jnp.arange(n_x)[:, None] == x
    own = jnp.sum(jnp.where(column[None, :, :, None] & column.T[None, :, :, None], table, 0), (1, 2))
    own = jnp.broadcast_to(own[:, None, :], (n_z, n_x, NCAP)).reshape(-1)
    there = n_z * R + (dx - 1) * (n_z * NCAP) + dz * NCAP + c
    where = jnp.where(dx == 0, dz * R + own, there).astype(jnp.int32)

    pieces, spots = [], []
    for d in range(n_z):
        pieces.append(blocks[d])
        spots.append([(0, R, d * R)])
    for j, step in enumerate(STEPS):
        base = n_z * R + ((-step) % n_x - 1) * (n_z * NCAP)
        for k in range(half + 1):
            pieces.append(sent[k][j])
            if k in (0, half):
                spots.append([(0, NCAP, base + k * NCAP)])
            else:
                spots.append([(0, NCAP, base + (n_z - k) * NCAP), (NCAP, NCAP, base + k * NCAP)])
    return pieces, spots, where, asks[:, 0]


def tiles_kernel(spots, first, cols_ref, slots_ref, places_ref, where_ref, a_ref, pt_ref, *refs):
    piece_refs, (out_ref, b_ref, near_ref, sems) = refs[: len(spots)], refs[len(spots) :]
    row = pl.program_id(0)
    width = b_ref.shape[-1]
    rows_of = pl.ds(row * BLOCK, BLOCK)

    @pl.when(row == 0)
    def _():
        copies = []
        for piece_ref, parts in zip(piece_refs, spots):
            for start, n, place in parts:
                copies.append(
                    pltpu.make_async_copy(
                        piece_ref.at[pl.ds(start, n), :, pl.ds(first, width)],
                        b_ref.at[pl.ds(place, n)],
                        sems.at[len(copies)],
                    )
                )
                copies[-1].start()

        @pl.loop(0, LT)
        def _(t):
            near_ref[t] = jnp.zeros(near_ref.shape[1:], jnp.float32)

        for copy in copies:
            copy.wait()

    lane = lax.broadcasted_iota(jnp.int32, (BLOCK, PAIR), 1)
    left = jnp.where(lane < BLOCK, 1.0, 0.0).astype(jnp.bfloat16)
    right = jnp.where(lane < BLOCK, 0.0, 1.0).astype(jnp.bfloat16)

    def target(k):
        return jnp.where(cols_ref[row, k] < 0, LT, slots_ref[row, k])

    def panel(k):
        return b_ref[where_ref[jnp.maximum(cols_ref[row, k], 0)]]

    def add(k, product):
        rounded = product.astype(jnp.bfloat16).astype(jnp.float32)
        near_ref[target(k), rows_of, :] += rounded

    for j in range(K // 2):
        pair = a_ref[0, :, j * PAIR : (j + 1) * PAIR]
        both = jnp.concatenate([pair * left, pair * right], axis=0)
        panels = jnp.concatenate([panel(2 * j), panel(2 * j + 1)], axis=0)
        product = jnp.dot(both, panels, preferred_element_type=jnp.float32)
        add(2 * j, product[:BLOCK])
        add(2 * j + 1, product[BLOCK:])
    last = a_ref[0, :, (K - 1) * BLOCK :]
    add(K - 1, jnp.dot(last, panel(K - 1), preferred_element_type=jnp.float32))

    @pl.when(row == R - 1)
    def _():
        beside = W // width

        @pl.loop(0, LT // beside)
        def _(u):
            near = jnp.concatenate([near_ref[u * beside + i] for i in range(beside)], axis=1)
            high = near.astype(jnp.bfloat16)
            low = (near - high.astype(jnp.float32)).astype(jnp.bfloat16)
            tile = jnp.dot(pt_ref[...], high, preferred_element_type=jnp.float32)
            tile += jnp.dot(pt_ref[...], low, preferred_element_type=jnp.float32)
            tile = tile.astype(jnp.bfloat16)
            for i in range(beside):
                out_ref[places_ref[u * beside + i]] = tile[:, i * width : (i + 1) * width]


def device_tiles(blocks, pt, pieces, spots, where, cols, slots, places, n_places, first, width):
    n_copies = sum(len(parts) for parts in spots)
    n_panels = max(place + n for parts in spots for _, n, place in parts)
    return pl.pallas_call(
        functools.partial(tiles_kernel, spots, first),
        out_shape=jax.ShapeDtypeStruct((n_places, W, width), jnp.bfloat16),
        grid_spec=pltpu.PrefetchScalarGridSpec(
            num_scalar_prefetch=4,
            grid=(R,),
            in_specs=[
                pl.BlockSpec((1, BLOCK, K * BLOCK), lambda i, *_: (i, 0, 0)),
                pl.BlockSpec((W, R * BLOCK), lambda i, *_: (0, 0)),
            ]
            + [pl.BlockSpec(memory_space=pltpu.HBM)] * len(pieces),
            out_specs=pl.BlockSpec((n_places, W, width), lambda i, *_: (0, 0, 0)),
            scratch_shapes=[
                pltpu.VMEM((n_panels, BLOCK, width), jnp.bfloat16),
                pltpu.VMEM((LT + 1, R * BLOCK, width), jnp.float32),
                pltpu.SemaphoreType.DMA((n_copies,)),
            ],
        ),
        compiler_params=pltpu.CompilerParams(
            dimension_semantics=("arbitrary",), vmem_limit_bytes=60 << 20
        ),
        cost_estimate=pl.CostEstimate(
            flops=8_000_000_000 * width // W,
            bytes_accessed=20_000_000 * width // W,
            transcendentals=0,
        ),
        name="device_tiles",
    )(cols, slots, places, where, blocks, pt, *pieces)


def table_kernel(labels_ref, got_ref, *refs):
    out_refs, sum_ref = refs[:-1], refs[-1]
    spread = sum_ref.shape[0] - 1
    each = spread // len(out_refs)

    @pl.loop(0, spread)
    def _(t):
        sum_ref[t] = jnp.zeros(sum_ref.shape[1:], jnp.float32)

    @pl.loop(0, got_ref.shape[0])
    def _(s):
        label = labels_ref[s]
        at = jnp.where(label < 0, spread, label)
        sum_ref[at] += got_ref[s].astype(jnp.float32)

    for i, out_ref in enumerate(out_refs):

        @pl.loop(0, each)
        def _(t):
            out_ref[t] = sum_ref[i * each + t].astype(out_ref.dtype)


def table_of(labels, got, spread, pieces):
    n, _, width = got.shape
    rows, each = 64, spread // pieces
    return pl.pallas_call(
        table_kernel,
        out_shape=[jax.ShapeDtypeStruct((each, W, width), jnp.bfloat16)] * pieces,
        grid_spec=pltpu.PrefetchScalarGridSpec(
            num_scalar_prefetch=1,
            grid=(W // rows,),
            in_specs=[pl.BlockSpec((n, rows, width), lambda i, *_: (0, i, 0))],
            out_specs=[pl.BlockSpec((each, rows, width), lambda i, *_: (0, i, 0))] * pieces,
            scratch_shapes=[pltpu.VMEM((spread + 1, rows, width), jnp.float32)],
        ),
        compiler_params=pltpu.CompilerParams(dimension_semantics=("arbitrary",)),
        cost_estimate=pl.CostEstimate(
            flops=n * W * width, bytes_accessed=6_000_000 * width // W, transcendentals=0
        ),
        name="table_of",
    )(labels, got)


def sum_over_groups(labels, got, spread, spread_out):
    groups = lax.axis_size("grp")
    if not spread_out:
        (table,) = table_of(labels, got, spread, 1)
        parts = lax.all_to_all(table, "grp", split_axis=0, concat_axis=0, tiled=True)
        parts = parts.reshape(groups, CT, W, got.shape[-1])
        return parts.astype(jnp.float32).sum(0)
    from_here = (labels - lax.axis_index("grp") * CT) % spread
    pieces = table_of(jnp.where(labels < 0, -1, from_here), got, spread, groups)
    total = pieces[0].astype(jnp.float32)
    for i in range(1, groups):
        pairs = [(g, (g + i) % groups) for g in range(groups)]
        total += lax.ppermute(pieces[i], "grp", pairs).astype(jnp.float32)
    return total


def layer(blocks, prolong, block_cols, fetch_rows, tile_slot, tile_owner, tile_place):
    dev_count = lax.axis_size("dev")
    grp_count = lax.axis_size("grp")
    panels = prolong[0, 0]
    owners = tile_owner[0, 0]
    dev_target = owners % dev_count
    label = (owners // dev_count) * CT + tile_place[0, 0]
    meant = dev_target[None, :] == jnp.arange(dev_count)[:, None]
    labels = jnp.max(jnp.where(meant, label[None, :], -1), axis=1)
    pieces, spots, where, got_labels = fetch(panels, fetch_rows[0, 0], labels)

    pt = panels.reshape(R * BLOCK, W).T
    parts = []
    width = W // HALVES
    for h in range(HALVES):
        sending = device_tiles(
            blocks[0, 0], pt, pieces, spots, where, block_cols[0, 0], tile_slot[0, 0],
            dev_target, dev_count, h * width, width,
        )
        got = lax.all_to_all(sending, "dev", split_axis=0, concat_axis=0, tiled=True)
        last = h == HALVES - 1
        parts.append(sum_over_groups(got_labels, got, grp_count * CT, not last))
    return jnp.concatenate(parts, axis=-1).reshape(1, 1, CT, W, W)


def solution(mesh):
    return jax.shard_map(
        layer,
        mesh=mesh,
        in_specs=(
            P("grp", "dev", None, None, None),
            P("grp", "dev", None, None, None),
            P("grp", "dev", None, None),
            P("grp", "dev", None, None),
            P("grp", "dev", None, None),
            P("grp", "dev", None),
            P("grp", "dev", None),
        ),
        out_specs=P("grp", "dev", None, None, None),
        check_vma=False,
    )
```

```python
import functools

import jax
import jax.numpy as jnp
from jax import lax
from jax.experimental import pallas as pl
from jax.experimental.pallas import tpu as pltpu
from jax.sharding import PartitionSpec as P


BLOCK = 64
W = 256
R = 12
K = 27
CT = 2
NCAP = 3
LT = 16
PAIR = 2 * BLOCK
STEPS = (1, -1, 2, 0)


def pick_kernel(n_x, ups, asks_ref, *refs):
    block_refs, out_refs = refs[: len(ups)], refs[len(ups) :]
    z, x = lax.axis_index("dev") // n_x, lax.axis_index("dev") % n_x
    n_z = asks_ref.shape[0] // n_x
    for i, (up, block_ref) in enumerate(zip(ups, block_refs)):
        source = (z + n_z - up) % n_z * n_x + x
        for step, out_ref in zip(STEPS, out_refs):
            peer = (x + n_x + step) % n_x
            for c in range(NCAP):
                out_ref[i * NCAP + c] = block_ref[asks_ref[source, 1 + peer * NCAP + c]]


def pick(asks, n_x, ups, blocks):
    shape = (len(blocks) * NCAP,) + blocks[0].shape[1:]
    vmem = pl.BlockSpec(memory_space=pltpu.VMEM)
    return pl.pallas_call(
        functools.partial(pick_kernel, n_x, ups),
        out_shape=[jax.ShapeDtypeStruct(shape, blocks[0].dtype)] * len(STEPS),
        in_specs=[pl.BlockSpec(memory_space=pltpu.SMEM)] + [vmem] * len(blocks),
        out_specs=[vmem] * len(STEPS),
        compiler_params=pltpu.CompilerParams(vmem_limit_bytes=16 << 20),
        cost_estimate=pl.CostEstimate(flops=0, bytes_accessed=1_500_000, transcendentals=0),
        name="pick",
    )(asks, *blocks)


def fetch(panels, rows_of, labels):
    n_z, n_x = 8, 4
    half = n_z // 2
    me = lax.axis_index("dev")
    z, x = me // n_x, me % n_x

    def along_z(step):
        return [(s, (s // n_x + step) % n_z * n_x + s % n_x) for s in range(n_z * n_x)]

    def along_x(step):
        return [(s, s // n_x * n_x + (s % n_x + step) % n_x) for s in range(n_z * n_x)]

    pieces, spots = [], []

    def forward(ups, blocks):
        picked = pick(asks, n_x, ups, blocks)
        for step, block in zip(STEPS, picked):
            if step:
                block = lax.ppermute(block, "dev", along_x(step))
            pieces.append(block)
            base = (-step) % n_x * n_z
            spots.append([(i * NCAP, NCAP, (base + -up % n_z) * NCAP) for i, up in enumerate(ups)])

    fetched = rows_of.reshape(n_z, 1, n_x * NCAP)
    asked = jnp.broadcast_to(fetched, (n_z, n_x, n_x * NCAP)).reshape(n_z * n_x, n_x * NCAP)
    asked = jnp.concatenate([labels[:, None], asked], axis=1)

    up = lax.ppermute(panels, "dev", along_z(1))
    down = lax.ppermute(panels, "dev", along_z(-1))
    asks = lax.all_to_all(asked, "dev", split_axis=0, concat_axis=0, tiled=True)
    for k in range(1, half):
        if k + 1 < half:
            new_up = lax.ppermute(up, "dev", along_z(1))
            new_down = lax.ppermute(down, "dev", along_z(-1))
        else:
            odd = lax.axis_index("grp") % 2 == 1
            n = n_z * n_x
            pairs = [
                (g * n + s, g * n + t)
                for g in range(lax.axis_size("grp"))
                for s, t in along_z(-1 if g % 2 else 1)
            ]
            far = lax.ppermute(jnp.where(odd, down, up), ("grp", "dev"), pairs)
        if k == 1:
            forward((0, k, -k), (panels, up, down))
        else:
            forward((k, -k), (up, down))
        up, down = new_up, new_down
    forward((half,), (far,))

    entry = jnp.arange(n_z * n_x * NCAP, dtype=jnp.int32)
    s, c = entry // NCAP, entry % NCAP
    dz, dx = (s // n_x - z) % n_z, (s % n_x - x) % n_x
    where = ((dx * n_z + dz) * NCAP + c).astype(jnp.int32)
    return pieces, spots, where, asks[:, 0]


def tiles_kernel(spots, cols_ref, slots_ref, places_ref, where_ref, a_hbm, pt_ref, *refs):
    piece_refs, (out_ref, a_ref, b_ref, near_ref, a_sems) = refs[: len(spots)], refs[len(spots) :]

    def load(row):
        return pltpu.make_async_copy(a_hbm.at[row], a_ref.at[row], a_sems.at[row])

    for row in range(R):
        load(row).start()
    for piece_ref, parts in zip(piece_refs, spots):
        for start, n, place in parts:
            for i in range(n):
                b_ref[place + i] = piece_ref[start + i]

    @pl.loop(0, LT)
    def _(t):
        near_ref[t] = jnp.zeros(near_ref.shape[1:], jnp.float32)

    lane = lax.broadcasted_iota(jnp.int32, (BLOCK, PAIR), 1)
    left = jnp.where(lane < BLOCK, 1.0, 0.0).astype(jnp.bfloat16)
    right = jnp.where(lane < BLOCK, 0.0, 1.0).astype(jnp.bfloat16)

    @pl.loop(0, R)
    def _(row):
        load(row).wait()
        rows_of = pl.ds(row * BLOCK, BLOCK)

        def target(k):
            return jnp.where(cols_ref[row, k] < 0, LT, slots_ref[row, k])

        def panel(k):
            return b_ref[where_ref[jnp.maximum(cols_ref[row, k], 0)]]

        def add(k, product):
            rounded = product.astype(jnp.bfloat16).astype(jnp.float32)
            near_ref[target(k), rows_of, :] += rounded

        for j in range(K // 2):
            pair = a_ref[row, :, j * PAIR : (j + 1) * PAIR]
            both = jnp.concatenate([pair * left, pair * right], axis=0)
            panels = jnp.concatenate([panel(2 * j), panel(2 * j + 1)], axis=0)
            product = jnp.dot(both, panels, preferred_element_type=jnp.float32)
            add(2 * j, product[:BLOCK])
            add(2 * j + 1, product[BLOCK:])
        last = a_ref[row, :, (K - 1) * BLOCK :]
        add(K - 1, jnp.dot(last, panel(K - 1), preferred_element_type=jnp.float32))

    @pl.loop(0, LT)
    def _(t):
        near = near_ref[t]
        high = near.astype(jnp.bfloat16)
        low = (near - high.astype(jnp.float32)).astype(jnp.bfloat16)
        tile = jnp.dot(pt_ref[...], high, preferred_element_type=jnp.float32)
        tile += jnp.dot(pt_ref[...], low, preferred_element_type=jnp.float32)
        out_ref[places_ref[t]] = tile.astype(jnp.bfloat16)


def device_tiles(blocks, pt, pieces, spots, where, cols, slots, places, n_places):
    n_panels = max(place + n for parts in spots for _, n, place in parts)
    smem, vmem = pl.BlockSpec(memory_space=pltpu.SMEM), pl.BlockSpec(memory_space=pltpu.VMEM)
    hbm = pl.BlockSpec(memory_space=pltpu.HBM)
    return pl.pallas_call(
        functools.partial(tiles_kernel, spots),
        out_shape=jax.ShapeDtypeStruct((n_places, W, W), jnp.bfloat16),
        in_specs=[smem] * 4 + [hbm, vmem] + [vmem] * len(pieces),
        out_specs=vmem,
        scratch_shapes=[
            pltpu.VMEM((R, BLOCK, K * BLOCK), jnp.bfloat16),
            pltpu.VMEM((n_panels, BLOCK, W), jnp.bfloat16),
            pltpu.VMEM((LT + 1, R * BLOCK, W), jnp.float32),
            pltpu.SemaphoreType.DMA((R,)),
        ],
        compiler_params=pltpu.CompilerParams(vmem_limit_bytes=50 << 20),
        cost_estimate=pl.CostEstimate(
            flops=8_000_000_000, bytes_accessed=12_000_000, transcendentals=0
        ),
        name="device_tiles",
    )(cols, slots, places, where, blocks, pt, *pieces)


def table_kernel(labels_ref, got_ref, here_ref, there_ref, sum_ref):
    n_here, n_there = here_ref.shape[0], there_ref.shape[0]

    @pl.loop(0, n_here + n_there)
    def _(t):
        sum_ref[t] = jnp.zeros(sum_ref.shape[1:], jnp.float32)

    @pl.loop(0, got_ref.shape[0])
    def _(s):
        label = labels_ref[s]
        at = jnp.where(label < 0, n_here + n_there, label)
        sum_ref[at] += got_ref[s].astype(jnp.float32)

    @pl.loop(0, n_here)
    def _(t):
        here_ref[t] = sum_ref[t]

    @pl.loop(0, n_there)
    def _(t):
        there_ref[t] = sum_ref[n_here + t].astype(there_ref.dtype)


def table_of(labels, got, n_here, n_there):
    rows = 64
    block = lambda n: pl.BlockSpec((n, rows, W), lambda i, *_: (0, i, 0))
    return pl.pallas_call(
        table_kernel,
        out_shape=[
            jax.ShapeDtypeStruct((n_here, W, W), jnp.float32),
            jax.ShapeDtypeStruct((n_there, W, W), jnp.bfloat16),
        ],
        grid_spec=pltpu.PrefetchScalarGridSpec(
            num_scalar_prefetch=1,
            grid=(W // rows,),
            in_specs=[block(got.shape[0])],
            out_specs=[block(n_here), block(n_there)],
            scratch_shapes=[pltpu.VMEM((n_here + n_there + 1, rows, W), jnp.float32)],
        ),
        compiler_params=pltpu.CompilerParams(dimension_semantics=("arbitrary",)),
        cost_estimate=pl.CostEstimate(flops=2_000_000, bytes_accessed=7_000_000, transcendentals=0),
        name="table_of",
    )(labels, got)


def sum_over_groups(labels, got):
    groups, cores = lax.axis_size("grp"), 2
    n_y = groups // cores
    y, core = lax.axis_index("grp") // cores, lax.axis_index("grp") % cores
    to, place = labels // CT, labels % CT
    dy = (to // cores - y) % n_y
    other = (to % cores - core) % cores
    at = jnp.where(labels < 0, -1, (other * n_y + dy) * CT + place)
    here, there = table_of(at, got, n_y * CT, n_y * CT)
    swap = [(g, g // cores * cores + (g + 1) % cores) for g in range(groups)]
    here += lax.ppermute(there, "grp", swap).astype(jnp.float32)
    total = here[:CT]
    for step in (2, 1, 3):
        pairs = [(g, (g + step * cores) % groups) for g in range(groups)]
        part = here[step * CT : (step + 1) * CT].astype(jnp.bfloat16)
        total += lax.ppermute(part, "grp", pairs).astype(jnp.float32)
    return total


def layer(blocks, prolong, block_cols, fetch_rows, tile_slot, tile_owner, tile_place):
    dev_count = lax.axis_size("dev")
    panels = prolong[0, 0]
    owners = tile_owner[0, 0]
    dev_target = owners % dev_count
    label = (owners // dev_count) * CT + tile_place[0, 0]
    meant = dev_target[None, :] == jnp.arange(dev_count)[:, None]
    labels = jnp.max(jnp.where(meant, label[None, :], -1), axis=1)
    pieces, spots, where, got_labels = fetch(panels, fetch_rows[0, 0], labels)

    pt = panels.reshape(R * BLOCK, W).T
    sending = device_tiles(
        blocks[0, 0], pt, pieces, spots, where, block_cols[0, 0], tile_slot[0, 0], dev_target, dev_count
    )
    got = lax.all_to_all(sending, "dev", split_axis=0, concat_axis=0, tiled=True)
    return sum_over_groups(got_labels, got).reshape(1, 1, CT, W, W)


def solution(mesh):
    return jax.shard_map(
        layer,
        mesh=mesh,
        in_specs=(
            P("grp", "dev", None, None, None),
            P("grp", "dev", None, None, None),
            P("grp", "dev", None, None),
            P("grp", "dev", None, None),
            P("grp", "dev", None, None),
            P("grp", "dev", None),
            P("grp", "dev", None),
        ),
        out_specs=P("grp", "dev", None, None, None),
        check_vma=False,
    )
```

```python
import functools

import jax
import jax.numpy as jnp
from jax import lax
from jax.experimental import pallas as pl
from jax.experimental.pallas import tpu as pltpu
from jax.sharding import PartitionSpec as P


BLOCK = 64
W = 256
R = 12
K = 27
CT = 2
NCAP = 3
LT = 16
PAIR = 2 * BLOCK
STEPS = (1, -1, 2, 0)


def pick_kernel(n_x, ups, asks_ref, *refs):
    block_refs, out_refs = refs[: len(ups)], refs[len(ups) :]
    z, x = lax.axis_index("dev") // n_x, lax.axis_index("dev") % n_x
    n_z = asks_ref.shape[0] // n_x
    for i, (up, block_ref) in enumerate(zip(ups, block_refs)):
        source = (z + n_z - up) % n_z * n_x + x
        for step, out_ref in zip(STEPS, out_refs):
            peer = (x + n_x + step) % n_x
            for c in range(NCAP):
                out_ref[i * NCAP + c] = block_ref[asks_ref[source, 1 + peer * NCAP + c]]


def pick(asks, n_x, ups, blocks):
    shape = (len(blocks) * NCAP,) + blocks[0].shape[1:]
    vmem = pl.BlockSpec(memory_space=pltpu.VMEM)
    return pl.pallas_call(
        functools.partial(pick_kernel, n_x, ups),
        out_shape=[jax.ShapeDtypeStruct(shape, blocks[0].dtype)] * len(STEPS),
        in_specs=[pl.BlockSpec(memory_space=pltpu.SMEM)] + [vmem] * len(blocks),
        out_specs=[vmem] * len(STEPS),
        compiler_params=pltpu.CompilerParams(vmem_limit_bytes=16 << 20),
        cost_estimate=pl.CostEstimate(flops=0, bytes_accessed=1_500_000, transcendentals=0),
        name="pick",
    )(asks, *blocks)


def fetch(panels, rows_of, labels):
    n_z, n_x = 8, 4
    half = n_z // 2
    me = lax.axis_index("dev")
    z, x = me // n_x, me % n_x

    def along_z(step):
        return [(s, (s // n_x + step) % n_z * n_x + s % n_x) for s in range(n_z * n_x)]

    def along_x(step):
        return [(s, s // n_x * n_x + (s % n_x + step) % n_x) for s in range(n_z * n_x)]

    pieces, spots = [], []

    def forward(ups, blocks):
        picked = pick(asks, n_x, ups, blocks)
        for step, block in zip(STEPS, picked):
            if step:
                block = lax.ppermute(block, "dev", along_x(step))
            pieces.append(block)
            base = (-step) % n_x * n_z
            spots.append([(i * NCAP, NCAP, (base + -up % n_z) * NCAP) for i, up in enumerate(ups)])

    fetched = rows_of.reshape(n_z, 1, n_x * NCAP)
    asked = jnp.broadcast_to(fetched, (n_z, n_x, n_x * NCAP)).reshape(n_z * n_x, n_x * NCAP)
    asked = jnp.concatenate([labels[:, None], asked], axis=1)

    asks = lax.all_to_all(asked, "dev", split_axis=0, concat_axis=0, tiled=True)
    up = lax.ppermute(panels, "dev", along_z(1))
    down = lax.ppermute(panels, "dev", along_z(-1))
    forward((0,), (panels,))
    for k in range(1, half):
        if k + 1 < half:
            new_up = lax.ppermute(up, "dev", along_z(1))
            new_down = lax.ppermute(down, "dev", along_z(-1))
        else:
            odd = lax.axis_index("grp") % 2 == 1
            n = n_z * n_x
            pairs = [
                (g * n + s, g * n + t)
                for g in range(lax.axis_size("grp"))
                for s, t in along_z(-1 if g % 2 else 1)
            ]
            far = lax.ppermute(jnp.where(odd, down, up), ("grp", "dev"), pairs)
        forward((k, -k), (up, down))
        up, down = new_up, new_down
    forward((half,), (far,))

    entry = jnp.arange(n_z * n_x * NCAP, dtype=jnp.int32)
    s, c = entry // NCAP, entry % NCAP
    dz, dx = (s // n_x - z) % n_z, (s % n_x - x) % n_x
    where = ((dx * n_z + dz) * NCAP + c).astype(jnp.int32)
    return pieces, spots, where, asks[:, 0]


def tiles_kernel(spots, cols_ref, slots_ref, places_ref, where_ref, a_hbm, pt_ref, *refs):
    piece_refs, (out_ref, a_ref, b_ref, near_ref, a_sems, b_sems) = refs[: len(spots)], refs[len(spots) :]

    def load(row):
        return pltpu.make_async_copy(a_hbm.at[row], a_ref.at[row], a_sems.at[row])

    for row in range(R):
        load(row).start()
    copies = []
    for piece_ref, parts in zip(piece_refs, spots):
        for start, n, place in parts:
            from_ref, to_ref = piece_ref.at[pl.ds(start, n)], b_ref.at[pl.ds(place, n)]
            copies.append(pltpu.make_async_copy(from_ref, to_ref, b_sems.at[len(copies)]))
            copies[-1].start()

    @pl.loop(0, LT)
    def _(t):
        near_ref[t] = jnp.zeros(near_ref.shape[1:], jnp.float32)

    for copy in copies:
        copy.wait()

    lane = lax.broadcasted_iota(jnp.int32, (BLOCK, PAIR), 1)
    left = jnp.where(lane < BLOCK, 1.0, 0.0).astype(jnp.bfloat16)
    right = jnp.where(lane < BLOCK, 0.0, 1.0).astype(jnp.bfloat16)

    @pl.loop(0, R)
    def _(row):
        load(row).wait()
        rows_of = pl.ds(row * BLOCK, BLOCK)

        def target(k):
            return jnp.where(cols_ref[row, k] < 0, LT, slots_ref[row, k])

        def panel(k):
            return b_ref[where_ref[jnp.maximum(cols_ref[row, k], 0)]]

        def add(k, product):
            rounded = product.astype(jnp.bfloat16).astype(jnp.float32)
            near_ref[target(k), rows_of, :] += rounded

        for j in range(K // 2):
            pair = a_ref[row, :, j * PAIR : (j + 1) * PAIR]
            both = jnp.concatenate([pair * left, pair * right], axis=0)
            panels = jnp.concatenate([panel(2 * j), panel(2 * j + 1)], axis=0)
            product = jnp.dot(both, panels, preferred_element_type=jnp.float32)
            add(2 * j, product[:BLOCK])
            add(2 * j + 1, product[BLOCK:])
        last = a_ref[row, :, (K - 1) * BLOCK :]
        add(K - 1, jnp.dot(last, panel(K - 1), preferred_element_type=jnp.float32))

    @pl.loop(0, LT)
    def _(t):
        near = near_ref[t]
        high = near.astype(jnp.bfloat16)
        low = (near - high.astype(jnp.float32)).astype(jnp.bfloat16)
        tile = jnp.dot(pt_ref[...], high, preferred_element_type=jnp.float32)
        tile += jnp.dot(pt_ref[...], low, preferred_element_type=jnp.float32)
        out_ref[places_ref[t]] = tile.astype(jnp.bfloat16)


def device_tiles(blocks, pt, pieces, spots, where, cols, slots, places, n_places):
    n_panels = max(place + n for parts in spots for _, n, place in parts)
    smem, vmem = pl.BlockSpec(memory_space=pltpu.SMEM), pl.BlockSpec(memory_space=pltpu.VMEM)
    hbm = pl.BlockSpec(memory_space=pltpu.HBM)
    return pl.pallas_call(
        functools.partial(tiles_kernel, spots),
        out_shape=jax.ShapeDtypeStruct((n_places, W, W), jnp.bfloat16),
        in_specs=[smem] * 4 + [hbm, vmem] + [pl.BlockSpec(memory_space=pl.ANY)] * len(pieces),
        out_specs=vmem,
        scratch_shapes=[
            pltpu.VMEM((R, BLOCK, K * BLOCK), jnp.bfloat16),
            pltpu.VMEM((n_panels, BLOCK, W), jnp.bfloat16),
            pltpu.VMEM((LT + 1, R * BLOCK, W), jnp.float32),
            pltpu.SemaphoreType.DMA((R,)),
            pltpu.SemaphoreType.DMA((sum(len(parts) for parts in spots),)),
        ],
        compiler_params=pltpu.CompilerParams(vmem_limit_bytes=51 << 20),
        cost_estimate=pl.CostEstimate(
            flops=8_000_000_000, bytes_accessed=12_000_000, transcendentals=0
        ),
        name="device_tiles",
    )(cols, slots, places, where, blocks, pt, *pieces)


def table_kernel(labels_ref, got_ref, *refs):
    here_refs, (there_ref, sum_ref) = refs[:-2], refs[-2:]
    n_here, n_there = len(here_refs) * CT, there_ref.shape[0]

    @pl.loop(0, n_here + n_there)
    def _(t):
        sum_ref[t] = jnp.zeros(sum_ref.shape[1:], jnp.float32)

    @pl.loop(0, got_ref.shape[0])
    def _(s):
        label = labels_ref[s]

        @pl.when(label >= 0)
        def _():
            sum_ref[label] += got_ref[s].astype(jnp.float32)

    for i, here_ref in enumerate(here_refs):
        for t in range(CT):
            here_ref[t] = sum_ref[i * CT + t]

    @pl.loop(0, n_there)
    def _(t):
        there_ref[t] = sum_ref[n_here + t].astype(there_ref.dtype)


def table_of(labels, got, n_here, n_there):
    rows = 64
    block = lambda n: pl.BlockSpec((n, rows, W), lambda i, *_: (0, i, 0))
    return pl.pallas_call(
        table_kernel,
        out_shape=[
            *[jax.ShapeDtypeStruct((CT, W, W), jnp.float32)] * (n_here // CT),
            jax.ShapeDtypeStruct((n_there, W, W), jnp.bfloat16),
        ],
        grid_spec=pltpu.PrefetchScalarGridSpec(
            num_scalar_prefetch=1,
            grid=(W // rows,),
            in_specs=[block(got.shape[0])],
            out_specs=[block(CT)] * (n_here // CT) + [block(n_there)],
            scratch_shapes=[pltpu.VMEM((n_here + n_there, rows, W), jnp.float32)],
        ),
        compiler_params=pltpu.CompilerParams(dimension_semantics=("arbitrary",)),
        cost_estimate=pl.CostEstimate(flops=2_000_000, bytes_accessed=7_000_000, transcendentals=0),
        name="table_of",
    )(labels, got)


def sum_over_groups(labels, got):
    groups, cores = lax.axis_size("grp"), 2
    n_y = groups // cores
    y, core = lax.axis_index("grp") // cores, lax.axis_index("grp") % cores
    to, place = labels // CT, labels % CT
    dy = (to // cores - y) % n_y
    other = (to % cores - core) % cores
    at = jnp.where(labels < 0, -1, (other * n_y + dy) * CT + place)
    *here, there = table_of(at, got, n_y * CT, n_y * CT)
    swap = [(g, g // cores * cores + (g + 1) % cores) for g in range(groups)]
    there = lax.ppermute(there, "grp", swap)

    def of_chip(step):
        return here[step] + there[step * CT : (step + 1) * CT].astype(jnp.float32)

    total = of_chip(0)
    for step in (2, 1, 3):
        pairs = [(g, (g + step * cores) % groups) for g in range(groups)]
        total += lax.ppermute(of_chip(step).astype(jnp.bfloat16), "grp", pairs).astype(jnp.float32)
    return total


def layer(blocks, prolong, block_cols, fetch_rows, tile_slot, tile_owner, tile_place):
    dev_count = lax.axis_size("dev")
    panels = prolong[0, 0]
    owners = tile_owner[0, 0]
    dev_target = owners % dev_count
    label = (owners // dev_count) * CT + tile_place[0, 0]
    meant = dev_target[None, :] == jnp.arange(dev_count)[:, None]
    labels = jnp.max(jnp.where(meant, label[None, :], -1), axis=1)
    pieces, spots, where, got_labels = fetch(panels, fetch_rows[0, 0], labels)

    pt = panels.reshape(R * BLOCK, W).T
    sending = device_tiles(
        blocks[0, 0], pt, pieces, spots, where, block_cols[0, 0], tile_slot[0, 0], dev_target, dev_count
    )
    got = lax.all_to_all(sending, "dev", split_axis=0, concat_axis=0, tiled=True)
    return sum_over_groups(got_labels, got).reshape(1, 1, CT, W, W)


def solution(mesh):
    return jax.shard_map(
        layer,
        mesh=mesh,
        in_specs=(
            P("grp", "dev", None, None, None),
            P("grp", "dev", None, None, None),
            P("grp", "dev", None, None),
            P("grp", "dev", None, None),
            P("grp", "dev", None, None),
            P("grp", "dev", None),
            P("grp", "dev", None),
        ),
        out_specs=P("grp", "dev", None, None, None),
        check_vma=False,
    )
```

```python
import functools

import jax
import jax.numpy as jnp
from jax import lax
from jax.experimental import pallas as pl
from jax.experimental.pallas import tpu as pltpu
from jax.sharding import PartitionSpec as P


BLOCK = 64
W = 256
R = 12
K = 27
CT = 2
NCAP = 3
LT = 16
PAIR = 2 * BLOCK
STEPS = (1, -1, 2, 0)


def pick_kernel(n_x, ups, asks_ref, *refs):
    block_refs, out_refs = refs[: len(ups)], refs[len(ups) :]
    z, x = lax.axis_index("dev") // n_x, lax.axis_index("dev") % n_x
    n_z = asks_ref.shape[0] // n_x
    for i, (up, block_ref) in enumerate(zip(ups, block_refs)):
        source = (z + n_z - up) % n_z * n_x + x
        for step, out_ref in zip(STEPS, out_refs):
            peer = (x + n_x + step) % n_x
            for c in range(NCAP):
                out_ref[i * NCAP + c] = block_ref[asks_ref[source, 1 + peer * NCAP + c]]


def pick(asks, n_x, ups, blocks):
    shape = (len(blocks) * NCAP,) + blocks[0].shape[1:]
    vmem = pl.BlockSpec(memory_space=pltpu.VMEM)
    return pl.pallas_call(
        functools.partial(pick_kernel, n_x, ups),
        out_shape=[jax.ShapeDtypeStruct(shape, blocks[0].dtype)] * len(STEPS),
        in_specs=[pl.BlockSpec(memory_space=pltpu.SMEM)] + [vmem] * len(blocks),
        out_specs=[vmem] * len(STEPS),
        compiler_params=pltpu.CompilerParams(vmem_limit_bytes=16 << 20),
        cost_estimate=pl.CostEstimate(flops=0, bytes_accessed=1_500_000, transcendentals=0),
        name="pick",
    )(asks, *blocks)


def fetch(panels, rows_of, labels):
    n_z, n_x = 8, 4
    half = n_z // 2
    me = lax.axis_index("dev")
    z, x = me // n_x, me % n_x

    def along_z(step):
        return [(s, (s // n_x + step) % n_z * n_x + s % n_x) for s in range(n_z * n_x)]

    def along_x(step):
        return [(s, s // n_x * n_x + (s % n_x + step) % n_x) for s in range(n_z * n_x)]

    pieces, spots = [], []

    def forward(asks, ups, blocks):
        picked = pick(asks, n_x, ups, blocks)
        for step, block in zip(STEPS, picked):
            if step:
                block = lax.ppermute(block, "dev", along_x(step))
            pieces.append(block)
            base = (-step) % n_x * n_z
            spots.append([(i * NCAP, NCAP, (base + -up % n_z) * NCAP) for i, up in enumerate(ups)])

    fetched = rows_of.reshape(n_z, 1, n_x * NCAP)
    asked = jnp.broadcast_to(fetched, (n_z, n_x, n_x * NCAP)).reshape(n_z * n_x, n_x * NCAP)
    asked = jnp.concatenate([labels[:, None], asked], axis=1)

    up = lax.ppermute(panels, "dev", along_z(1))
    down = lax.ppermute(panels, "dev", along_z(-1))
    asks = lax.all_to_all(asked, "dev", split_axis=0, concat_axis=0, tiled=True)
    forward(asked, (0,), (panels,))
    for k in range(1, half):
        if k + 1 < half:
            new_up = lax.ppermute(up, "dev", along_z(1))
            new_down = lax.ppermute(down, "dev", along_z(-1))
        else:
            odd = lax.axis_index("grp") % 2 == 1
            n = n_z * n_x
            pairs = [
                (g * n + s, g * n + t)
                for g in range(lax.axis_size("grp"))
                for s, t in along_z(-1 if g % 2 else 1)
            ]
            far = lax.ppermute(jnp.where(odd, down, up), ("grp", "dev"), pairs)
        forward(asks, (k, -k), (up, down))
        up, down = new_up, new_down
    forward(asks, (half,), (far,))

    entry = jnp.arange(n_z * n_x * NCAP, dtype=jnp.int32)
    s, c = entry // NCAP, entry % NCAP
    dz, dx = (s // n_x - z) % n_z, (s % n_x - x) % n_x
    where = ((dx * n_z + dz) * NCAP + c).astype(jnp.int32)
    return pieces, spots, where, asks[:, 0]


def tiles_kernel(spots, cols_ref, slots_ref, places_ref, where_ref, a_hbm, pt_ref, *refs):
    piece_refs, (out_ref, a_ref, b_ref, near_ref, a_sems) = refs[: len(spots)], refs[len(spots) :]

    def load(row):
        return pltpu.make_async_copy(a_hbm.at[row], a_ref.at[row], a_sems.at[row])

    for row in range(R):
        load(row).start()
    for piece_ref, parts in zip(piece_refs, spots):
        for start, n, place in parts:
            for i in range(n):
                b_ref[place + i] = piece_ref[start + i]

    @pl.loop(0, LT)
    def _(t):
        near_ref[t] = jnp.zeros(near_ref.shape[1:], jnp.float32)

    lane = lax.broadcasted_iota(jnp.int32, (BLOCK, PAIR), 1)
    left = jnp.where(lane < BLOCK, 1.0, 0.0).astype(jnp.bfloat16)
    right = jnp.where(lane < BLOCK, 0.0, 1.0).astype(jnp.bfloat16)

    @pl.loop(0, R)
    def _(row):
        load(row).wait()
        rows_of = pl.ds(row * BLOCK, BLOCK)

        def target(k):
            return jnp.where(cols_ref[row, k] < 0, LT, slots_ref[row, k])

        def panel(k):
            return b_ref[where_ref[jnp.maximum(cols_ref[row, k], 0)]]

        def add(k, product):
            rounded = product.astype(jnp.bfloat16).astype(jnp.float32)
            near_ref[target(k), rows_of, :] += rounded

        for j in range(K // 2):
            pair = a_ref[row, :, j * PAIR : (j + 1) * PAIR]
            both = jnp.concatenate([pair * left, pair * right], axis=0)
            panels = jnp.concatenate([panel(2 * j), panel(2 * j + 1)], axis=0)
            product = jnp.dot(both, panels, preferred_element_type=jnp.float32)
            add(2 * j, product[:BLOCK])
            add(2 * j + 1, product[BLOCK:])
        last = a_ref[row, :, (K - 1) * BLOCK :]
        add(K - 1, jnp.dot(last, panel(K - 1), preferred_element_type=jnp.float32))

    @pl.loop(0, LT)
    def _(t):
        near = near_ref[t]
        high = near.astype(jnp.bfloat16)
        low = (near - high.astype(jnp.float32)).astype(jnp.bfloat16)
        tile = jnp.dot(pt_ref[...], high, preferred_element_type=jnp.float32)
        tile += jnp.dot(pt_ref[...], low, preferred_element_type=jnp.float32)
        out_ref[places_ref[t]] = tile.astype(jnp.bfloat16)


def device_tiles(blocks, pt, pieces, spots, where, cols, slots, places, n_places):
    n_panels = max(place + n for parts in spots for _, n, place in parts)
    smem, vmem = pl.BlockSpec(memory_space=pltpu.SMEM), pl.BlockSpec(memory_space=pltpu.VMEM)
    hbm = pl.BlockSpec(memory_space=pltpu.HBM)
    return pl.pallas_call(
        functools.partial(tiles_kernel, spots),
        out_shape=jax.ShapeDtypeStruct((n_places, W, W), jnp.bfloat16),
        in_specs=[smem] * 4 + [hbm, vmem] + [vmem] * len(pieces),
        out_specs=vmem,
        scratch_shapes=[
            pltpu.VMEM((R, BLOCK, K * BLOCK), jnp.bfloat16),
            pltpu.VMEM((n_panels, BLOCK, W), jnp.bfloat16),
            pltpu.VMEM((LT + 1, R * BLOCK, W), jnp.float32),
            pltpu.SemaphoreType.DMA((R,)),
        ],
        compiler_params=pltpu.CompilerParams(vmem_limit_bytes=51 << 20),
        cost_estimate=pl.CostEstimate(
            flops=8_000_000_000, bytes_accessed=12_000_000, transcendentals=0
        ),
        name="device_tiles",
    )(cols, slots, places, where, blocks, pt, *pieces)


def table_kernel(first, labels_ref, got_ref, out_ref, sum_ref):
    n = sum_ref.shape[0]

    @pl.loop(0, n)
    def _(t):
        sum_ref[t] = jnp.zeros(sum_ref.shape[1:], jnp.float32)

    @pl.loop(0, got_ref.shape[0])
    def _(s):
        at = labels_ref[s] - first

        @pl.when((at >= 0) & (at < n))
        def _():
            sum_ref[at] += got_ref[s].astype(jnp.float32)

    @pl.loop(0, n)
    def _(t):
        out_ref[t] = sum_ref[t].astype(out_ref.dtype)


def table_of(labels, got, first, n, dtype):
    rows = 64
    block = lambda n: pl.BlockSpec((n, rows, W), lambda i, *_: (0, i, 0))
    return pl.pallas_call(
        functools.partial(table_kernel, first),
        out_shape=jax.ShapeDtypeStruct((n, W, W), dtype),
        grid_spec=pltpu.PrefetchScalarGridSpec(
            num_scalar_prefetch=1,
            grid=(W // rows,),
            in_specs=[block(got.shape[0])],
            out_specs=block(n),
            scratch_shapes=[pltpu.VMEM((n, rows, W), jnp.float32)],
        ),
        compiler_params=pltpu.CompilerParams(dimension_semantics=("arbitrary",)),
        cost_estimate=pl.CostEstimate(flops=1_000_000, bytes_accessed=6_000_000, transcendentals=0),
        name="table_of",
    )(labels, got)


def sum_over_groups(labels, got):
    groups, cores = lax.axis_size("grp"), 2
    n_y = groups // cores
    y, core = lax.axis_index("grp") // cores, lax.axis_index("grp") % cores
    to, place = labels // CT, labels % CT
    dy = (to // cores - y) % n_y
    other = (to % cores - core) % cores
    at = jnp.where(labels < 0, -1, (other * n_y + dy) * CT + place)
    n = n_y * CT
    there = table_of(at, got, n, n, jnp.bfloat16)
    swap = [(g, g // cores * cores + (g + 1) % cores) for g in range(groups)]
    there = lax.ppermute(there, "grp", swap)
    here = table_of(at, got, 0, n, jnp.float32)
    here += there.astype(jnp.float32)
    total = here[:CT]
    for step in (2, 1, 3):
        pairs = [(g, (g + step * cores) % groups) for g in range(groups)]
        part = here[step * CT : (step + 1) * CT].astype(jnp.bfloat16)
        total += lax.ppermute(part, "grp", pairs).astype(jnp.float32)
    return total


def layer(blocks, prolong, block_cols, fetch_rows, tile_slot, tile_owner, tile_place):
    dev_count = lax.axis_size("dev")
    panels = prolong[0, 0]
    owners = tile_owner[0, 0]
    dev_target = owners % dev_count
    label = (owners // dev_count) * CT + tile_place[0, 0]
    meant = dev_target[None, :] == jnp.arange(dev_count)[:, None]
    labels = jnp.max(jnp.where(meant, label[None, :], -1), axis=1)
    pieces, spots, where, got_labels = fetch(panels, fetch_rows[0, 0], labels)

    pt = panels.reshape(R * BLOCK, W).T
    sending = device_tiles(
        blocks[0, 0], pt, pieces, spots, where, block_cols[0, 0], tile_slot[0, 0], dev_target, dev_count
    )
    got = lax.all_to_all(sending, "dev", split_axis=0, concat_axis=0, tiled=True)
    return sum_over_groups(got_labels, got).reshape(1, 1, CT, W, W)


def solution(mesh):
    return jax.shard_map(
        layer,
        mesh=mesh,
        in_specs=(
            P("grp", "dev", None, None, None),
            P("grp", "dev", None, None, None),
            P("grp", "dev", None, None),
            P("grp", "dev", None, None),
            P("grp", "dev", None, None),
            P("grp", "dev", None),
            P("grp", "dev", None),
        ),
        out_specs=P("grp", "dev", None, None, None),
        check_vma=False,
    )
```

```python
import functools

import jax
import jax.numpy as jnp
from jax import lax
from jax.experimental import pallas as pl
from jax.experimental.pallas import tpu as pltpu
from jax.sharding import PartitionSpec as P


BLOCK = 64
W = 256
R = 12
K = 27
CT = 2
NCAP = 3
LT = 16
PAIR = 2 * BLOCK
STEPS = (1, -1, 2, 0)


def pick_kernel(n_x, ups, asks_ref, *refs):
    block_refs, out_refs = refs[: len(ups)], refs[len(ups) :]
    z, x = lax.axis_index("dev") // n_x, lax.axis_index("dev") % n_x
    n_z = asks_ref.shape[0] // n_x
    for i, (up, block_ref) in enumerate(zip(ups, block_refs)):
        source = (z + n_z - up) % n_z * n_x + x
        for step, out_ref in zip(STEPS, out_refs):
            peer = (x + n_x + step) % n_x
            for c in range(NCAP):
                out_ref[i * NCAP + c] = block_ref[asks_ref[source, 1 + peer * NCAP + c]]


def pick(asks, n_x, ups, blocks):
    shape = (len(blocks) * NCAP,) + blocks[0].shape[1:]
    vmem = pl.BlockSpec(memory_space=pltpu.VMEM)
    return pl.pallas_call(
        functools.partial(pick_kernel, n_x, ups),
        out_shape=[jax.ShapeDtypeStruct(shape, blocks[0].dtype)] * len(STEPS),
        in_specs=[pl.BlockSpec(memory_space=pltpu.SMEM)] + [vmem] * len(blocks),
        out_specs=[vmem] * len(STEPS),
        compiler_params=pltpu.CompilerParams(vmem_limit_bytes=16 << 20),
        cost_estimate=pl.CostEstimate(flops=0, bytes_accessed=1_500_000, transcendentals=0),
        name="pick",
    )(asks, *blocks)


def fetch(panels, rows_of, labels):
    n_z, n_x = 8, 4
    half = n_z // 2
    me = lax.axis_index("dev")
    z, x = me // n_x, me % n_x

    def along_z(step):
        return [(s, (s // n_x + step) % n_z * n_x + s % n_x) for s in range(n_z * n_x)]

    def along_x(step):
        return [(s, s // n_x * n_x + (s % n_x + step) % n_x) for s in range(n_z * n_x)]

    pieces, spots = [], []

    def forward(asks, ups, blocks):
        picked = pick(asks, n_x, ups, blocks)
        for step, block in zip(STEPS, picked):
            if step:
                block = lax.ppermute(block, "dev", along_x(step))
            pieces.append(block)
            base = (-step) % n_x * n_z
            spots.append([(i * NCAP, NCAP, (base + -up % n_z) * NCAP) for i, up in enumerate(ups)])

    fetched = rows_of.reshape(n_z, 1, n_x * NCAP)
    asked = jnp.broadcast_to(fetched, (n_z, n_x, n_x * NCAP)).reshape(n_z * n_x, n_x * NCAP)
    asked = jnp.concatenate([labels[:, None], asked], axis=1)

    up = lax.ppermute(panels, "dev", along_z(1))
    down = lax.ppermute(panels, "dev", along_z(-1))
    asks = lax.all_to_all(asked, "dev", split_axis=0, concat_axis=0, tiled=True)
    for k in range(1, half):
        if k + 1 < half:
            new_up = lax.ppermute(up, "dev", along_z(1))
            new_down = lax.ppermute(down, "dev", along_z(-1))
        else:
            odd = lax.axis_index("grp") % 2 == 1
            n = n_z * n_x
            pairs = [
                (g * n + s, g * n + t)
                for g in range(lax.axis_size("grp"))
                for s, t in along_z(-1 if g % 2 else 1)
            ]
            far = lax.ppermute(jnp.where(odd, down, up), ("grp", "dev"), pairs)
        if k == 1:
            forward(asks, (0, k, -k), (panels, up, down))
        else:
            forward(asks, (k, -k), (up, down))
        up, down = new_up, new_down
    forward(asks, (half,), (far,))

    entry = jnp.arange(n_z * n_x * NCAP, dtype=jnp.int32)
    s, c = entry // NCAP, entry % NCAP
    dz, dx = (s // n_x - z) % n_z, (s % n_x - x) % n_x
    where = ((dx * n_z + dz) * NCAP + c).astype(jnp.int32)
    return pieces, spots, where, asks[:, 0]


def tiles_kernel(spots, cols_ref, slots_ref, places_ref, where_ref, a_hbm, pt_ref, *refs):
    piece_refs, (out_ref, a_ref, b_ref, near_ref, a_sems) = refs[: len(spots)], refs[len(spots) :]

    def load(row):
        return pltpu.make_async_copy(a_hbm.at[row], a_ref.at[row], a_sems.at[row])

    for row in range(R):
        load(row).start()
    for piece_ref, parts in zip(piece_refs, spots):
        for start, n, place in parts:
            for i in range(n):
                b_ref[place + i] = piece_ref[start + i]

    @pl.loop(0, LT)
    def _(t):
        near_ref[t] = jnp.zeros(near_ref.shape[1:], jnp.float32)

    lane = lax.broadcasted_iota(jnp.int32, (BLOCK, PAIR), 1)
    left = jnp.where(lane < BLOCK, 1.0, 0.0).astype(jnp.bfloat16)
    right = jnp.where(lane < BLOCK, 0.0, 1.0).astype(jnp.bfloat16)

    @pl.loop(0, R)
    def _(row):
        load(row).wait()
        rows_of = pl.ds(row * BLOCK, BLOCK)

        def target(k):
            return jnp.where(cols_ref[row, k] < 0, LT, slots_ref[row, k])

        def panel(k):
            return b_ref[where_ref[jnp.maximum(cols_ref[row, k], 0)]]

        def add(k, product):
            rounded = product.astype(jnp.bfloat16).astype(jnp.float32)
            near_ref[target(k), rows_of, :] += rounded

        for j in range(K // 2):
            pair = a_ref[row, :, j * PAIR : (j + 1) * PAIR]
            both = jnp.concatenate([pair * left, pair * right], axis=0)
            panels = jnp.concatenate([panel(2 * j), panel(2 * j + 1)], axis=0)
            product = jnp.dot(both, panels, preferred_element_type=jnp.float32)
            add(2 * j, product[:BLOCK])
            add(2 * j + 1, product[BLOCK:])
        last = a_ref[row, :, (K - 1) * BLOCK :]
        add(K - 1, jnp.dot(last, panel(K - 1), preferred_element_type=jnp.float32))

    @pl.loop(0, LT)
    def _(t):
        near = near_ref[t]
        high = near.astype(jnp.bfloat16)
        low = (near - high.astype(jnp.float32)).astype(jnp.bfloat16)
        tile = jnp.dot(pt_ref[...], high, preferred_element_type=jnp.float32)
        tile += jnp.dot(pt_ref[...], low, preferred_element_type=jnp.float32)
        out_ref[places_ref[t]] = tile.astype(jnp.bfloat16)


def device_tiles(blocks, pt, pieces, spots, where, cols, slots, places, n_places):
    n_panels = max(place + n for parts in spots for _, n, place in parts)
    smem, vmem = pl.BlockSpec(memory_space=pltpu.SMEM), pl.BlockSpec(memory_space=pltpu.VMEM)
    hbm = pl.BlockSpec(memory_space=pltpu.HBM)
    return pl.pallas_call(
        functools.partial(tiles_kernel, spots),
        out_shape=jax.ShapeDtypeStruct((n_places, W, W), jnp.bfloat16),
        in_specs=[smem] * 4 + [hbm, vmem] + [vmem] * len(pieces),
        out_specs=vmem,
        scratch_shapes=[
            pltpu.VMEM((R, BLOCK, K * BLOCK), jnp.bfloat16),
            pltpu.VMEM((n_panels, BLOCK, W), jnp.bfloat16),
            pltpu.VMEM((LT + 1, R * BLOCK, W), jnp.float32),
            pltpu.SemaphoreType.DMA((R,)),
        ],
        compiler_params=pltpu.CompilerParams(vmem_limit_bytes=51 << 20),
        cost_estimate=pl.CostEstimate(
            flops=8_000_000_000, bytes_accessed=12_000_000, transcendentals=0
        ),
        name="device_tiles",
    )(cols, slots, places, where, blocks, pt, *pieces)


def table_kernel(labels_ref, got_hbm, here_ref, there_ref, got_ref, sum_ref, sems):
    n_here, n_there = here_ref.shape[0], there_ref.shape[0]

    def load(s):
        return pltpu.make_async_copy(got_hbm.at[s], got_ref.at[s], sems.at[s])

    @pl.loop(0, got_ref.shape[0])
    def _(s):
        @pl.when(labels_ref[s] >= 0)
        def _():
            load(s).start()

    @pl.loop(0, n_here)
    def _(t):
        here_ref[t] = jnp.zeros(here_ref.shape[1:], jnp.float32)

    @pl.loop(0, n_there)
    def _(t):
        sum_ref[t] = jnp.zeros(sum_ref.shape[1:], jnp.float32)

    @pl.loop(0, got_ref.shape[0])
    def _(s):
        label = labels_ref[s]

        @pl.when(label >= 0)
        def _():
            load(s).wait()

        @pl.when((label >= 0) & (label < n_here))
        def _():
            here_ref[label] += got_ref[s].astype(jnp.float32)

        @pl.when(label >= n_here)
        def _():
            sum_ref[label - n_here] += got_ref[s].astype(jnp.float32)

    @pl.loop(0, n_there)
    def _(t):
        there_ref[t] = sum_ref[t].astype(there_ref.dtype)


def table_of(labels, got, n_here, n_there):
    vmem = pl.BlockSpec(memory_space=pltpu.VMEM)
    return pl.pallas_call(
        table_kernel,
        out_shape=[
            jax.ShapeDtypeStruct((n_here, W, W), jnp.float32),
            jax.ShapeDtypeStruct((n_there, W, W), jnp.bfloat16),
        ],
        in_specs=[pl.BlockSpec(memory_space=pltpu.SMEM), pl.BlockSpec(memory_space=pltpu.HBM)],
        out_specs=[vmem] * 2,
        scratch_shapes=[
            pltpu.VMEM(got.shape, got.dtype),
            pltpu.VMEM((n_there, W, W), jnp.float32),
            pltpu.SemaphoreType.DMA((got.shape[0],)),
        ],
        compiler_params=pltpu.CompilerParams(vmem_limit_bytes=24 << 20),
        cost_estimate=pl.CostEstimate(flops=2_000_000, bytes_accessed=7_000_000, transcendentals=0),
        name="table_of",
    )(labels, got)


def sum_over_groups(labels, got):
    groups, cores = lax.axis_size("grp"), 2
    n_y = groups // cores
    y, core = lax.axis_index("grp") // cores, lax.axis_index("grp") % cores
    to, place = labels // CT, labels % CT
    dy = (to // cores - y) % n_y
    other = (to % cores - core) % cores
    at = jnp.where(labels < 0, -1, (other * n_y + dy) * CT + place)
    here, there = table_of(at, got, n_y * CT, n_y * CT)
    swap = [(g, g // cores * cores + (g + 1) % cores) for g in range(groups)]
    here += lax.ppermute(there, "grp", swap).astype(jnp.float32)
    total = here[:CT]
    for step in (2, 1, 3):
        pairs = [(g, (g + step * cores) % groups) for g in range(groups)]
        part = here[step * CT : (step + 1) * CT].astype(jnp.bfloat16)
        total += lax.ppermute(part, "grp", pairs).astype(jnp.float32)
    return total


def layer(blocks, prolong, block_cols, fetch_rows, tile_slot, tile_owner, tile_place):
    dev_count = lax.axis_size("dev")
    panels = prolong[0, 0]
    owners = tile_owner[0, 0]
    dev_target = owners % dev_count
    label = (owners // dev_count) * CT + tile_place[0, 0]
    meant = dev_target[None, :] == jnp.arange(dev_count)[:, None]
    labels = jnp.max(jnp.where(meant, label[None, :], -1), axis=1)
    pieces, spots, where, got_labels = fetch(panels, fetch_rows[0, 0], labels)

    pt = panels.reshape(R * BLOCK, W).T
    sending = device_tiles(
        blocks[0, 0], pt, pieces, spots, where, block_cols[0, 0], tile_slot[0, 0], dev_target, dev_count
    )
    got = lax.all_to_all(sending, "dev", split_axis=0, concat_axis=0, tiled=True)
    return sum_over_groups(got_labels, got).reshape(1, 1, CT, W, W)


def solution(mesh):
    return jax.shard_map(
        layer,
        mesh=mesh,
        in_specs=(
            P("grp", "dev", None, None, None),
            P("grp", "dev", None, None, None),
            P("grp", "dev", None, None),
            P("grp", "dev", None, None),
            P("grp", "dev", None, None),
            P("grp", "dev", None),
            P("grp", "dev", None),
        ),
        out_specs=P("grp", "dev", None, None, None),
        check_vma=False,
    )
```

```python
import functools

import jax
import jax.numpy as jnp
from jax import lax
from jax.experimental import pallas as pl
from jax.experimental.pallas import tpu as pltpu
from jax.sharding import PartitionSpec as P


BLOCK = 64
W = 256
R = 12
K = 27
CT = 2
NCAP = 3
LT = 16
PAIR = 2 * BLOCK
STEPS = (2, 1, -1, 0)


def pick_kernel(n_x, ups, asks_ref, *refs):
    block_refs, out_refs = refs[: len(ups)], refs[len(ups) :]
    z, x = lax.axis_index("dev") // n_x, lax.axis_index("dev") % n_x
    n_z = asks_ref.shape[0] // n_x
    for i, (up, block_ref) in enumerate(zip(ups, block_refs)):
        source = (z + n_z - up) % n_z * n_x + x
        for step, out_ref in zip(STEPS, out_refs):
            peer = (x + n_x + step) % n_x
            for c in range(NCAP):
                out_ref[i * NCAP + c] = block_ref[asks_ref[source, 1 + peer * NCAP + c]]


def pick(asks, n_x, ups, blocks):
    shape = (len(blocks) * NCAP,) + blocks[0].shape[1:]
    vmem = pl.BlockSpec(memory_space=pltpu.VMEM)
    return pl.pallas_call(
        functools.partial(pick_kernel, n_x, ups),
        out_shape=[jax.ShapeDtypeStruct(shape, blocks[0].dtype)] * len(STEPS),
        in_specs=[pl.BlockSpec(memory_space=pltpu.SMEM)] + [vmem] * len(blocks),
        out_specs=[vmem] * len(STEPS),
        compiler_params=pltpu.CompilerParams(vmem_limit_bytes=16 << 20),
        cost_estimate=pl.CostEstimate(flops=0, bytes_accessed=1_500_000, transcendentals=0),
        name="pick",
    )(asks, *blocks)


def fetch(panels, rows_of, labels):
    n_z, n_x = 8, 4
    half = n_z // 2
    me = lax.axis_index("dev")
    z, x = me // n_x, me % n_x

    def along_z(step):
        return [(s, (s // n_x + step) % n_z * n_x + s % n_x) for s in range(n_z * n_x)]

    def along_x(step):
        return [(s, s // n_x * n_x + (s % n_x + step) % n_x) for s in range(n_z * n_x)]

    pieces, spots = [], []

    def forward(asks, ups, blocks):
        picked = pick(asks, n_x, ups, blocks)
        for step, block in zip(STEPS, picked):
            if step:
                block = lax.ppermute(block, "dev", along_x(step))
            pieces.append(block)
            base = (-step) % n_x * n_z
            spots.append([(i * NCAP, NCAP, (base + -up % n_z) * NCAP) for i, up in enumerate(ups)])

    fetched = rows_of.reshape(n_z, 1, n_x * NCAP)
    asked = jnp.broadcast_to(fetched, (n_z, n_x, n_x * NCAP)).reshape(n_z * n_x, n_x * NCAP)
    asked = jnp.concatenate([labels[:, None], asked], axis=1)

    up = lax.ppermute(panels, "dev", along_z(1))
    down = lax.ppermute(panels, "dev", along_z(-1))
    asks = lax.all_to_all(asked, "dev", split_axis=0, concat_axis=0, tiled=True)
    forward(asked, (0,), (panels,))
    for k in range(1, half):
        if k + 1 < half:
            new_up = lax.ppermute(up, "dev", along_z(1))
            new_down = lax.ppermute(down, "dev", along_z(-1))
        else:
            odd = lax.axis_index("grp") % 2 == 1
            n = n_z * n_x
            pairs = [
                (g * n + s, g * n + t)
                for g in range(lax.axis_size("grp"))
                for s, t in along_z(-1 if g % 2 else 1)
            ]
            far = lax.ppermute(jnp.where(odd, down, up), ("grp", "dev"), pairs)
        forward(asks, (k, -k), (up, down))
        up, down = new_up, new_down
    forward(asks, (half,), (far,))

    entry = jnp.arange(n_z * n_x * NCAP, dtype=jnp.int32)
    s, c = entry // NCAP, entry % NCAP
    dz, dx = (s // n_x - z) % n_z, (s % n_x - x) % n_x
    where = ((dx * n_z + dz) * NCAP + c).astype(jnp.int32)
    return pieces, spots, where, asks[:, 0]


def tiles_kernel(spots, cols_ref, slots_ref, places_ref, where_ref, a_hbm, pt_ref, *refs):
    piece_refs, (out_ref, a_ref, b_ref, near_ref, a_sems) = refs[: len(spots)], refs[len(spots) :]

    def load(row):
        return pltpu.make_async_copy(a_hbm.at[row], a_ref.at[row], a_sems.at[row])

    for row in range(R):
        load(row).start()
    for piece_ref, parts in zip(piece_refs, spots):
        for start, n, place in parts:
            for i in range(n):
                b_ref[place + i] = piece_ref[start + i]

    @pl.loop(0, LT)
    def _(t):
        near_ref[t] = jnp.zeros(near_ref.shape[1:], jnp.float32)

    lane = lax.broadcasted_iota(jnp.int32, (BLOCK, PAIR), 1)
    left = jnp.where(lane < BLOCK, 1.0, 0.0).astype(jnp.bfloat16)
    right = jnp.where(lane < BLOCK, 0.0, 1.0).astype(jnp.bfloat16)

    @pl.loop(0, R)
    def _(row):
        load(row).wait()
        rows_of = pl.ds(row * BLOCK, BLOCK)

        def target(k):
            return jnp.where(cols_ref[row, k] < 0, LT, slots_ref[row, k])

        def panel(k):
            return b_ref[where_ref[jnp.maximum(cols_ref[row, k], 0)]]

        def add(k, product):
            rounded = product.astype(jnp.bfloat16).astype(jnp.float32)
            near_ref[target(k), rows_of, :] += rounded

        for j in range(K // 2):
            pair = a_ref[row, :, j * PAIR : (j + 1) * PAIR]
            both = jnp.concatenate([pair * left, pair * right], axis=0)
            panels = jnp.concatenate([panel(2 * j), panel(2 * j + 1)], axis=0)
            product = jnp.dot(both, panels, preferred_element_type=jnp.float32)
            add(2 * j, product[:BLOCK])
            add(2 * j + 1, product[BLOCK:])
        last = a_ref[row, :, (K - 1) * BLOCK :]
        add(K - 1, jnp.dot(last, panel(K - 1), preferred_element_type=jnp.float32))

    @pl.loop(0, LT)
    def _(t):
        near = near_ref[t]
        high = near.astype(jnp.bfloat16)
        low = (near - high.astype(jnp.float32)).astype(jnp.bfloat16)
        tile = jnp.dot(pt_ref[...], high, preferred_element_type=jnp.float32)
        tile += jnp.dot(pt_ref[...], low, preferred_element_type=jnp.float32)
        out_ref[places_ref[t]] = tile.astype(jnp.bfloat16)


def device_tiles(blocks, pt, pieces, spots, where, cols, slots, places, n_places):
    n_panels = max(place + n for parts in spots for _, n, place in parts)
    smem, vmem = pl.BlockSpec(memory_space=pltpu.SMEM), pl.BlockSpec(memory_space=pltpu.VMEM)
    hbm = pl.BlockSpec(memory_space=pltpu.HBM)
    return pl.pallas_call(
        functools.partial(tiles_kernel, spots),
        out_shape=jax.ShapeDtypeStruct((n_places, W, W), jnp.bfloat16),
        in_specs=[smem] * 4 + [hbm, vmem] + [vmem] * len(pieces),
        out_specs=vmem,
        scratch_shapes=[
            pltpu.VMEM((R, BLOCK, K * BLOCK), jnp.bfloat16),
            pltpu.VMEM((n_panels, BLOCK, W), jnp.bfloat16),
            pltpu.VMEM((LT + 1, R * BLOCK, W), jnp.float32),
            pltpu.SemaphoreType.DMA((R,)),
        ],
        compiler_params=pltpu.CompilerParams(vmem_limit_bytes=51 << 20),
        cost_estimate=pl.CostEstimate(
            flops=8_000_000_000, bytes_accessed=12_000_000, transcendentals=0
        ),
        name="device_tiles",
    )(cols, slots, places, where, blocks, pt, *pieces)


def table_kernel(labels_ref, got_hbm, here_ref, there_ref, got_ref, sum_ref, sems):
    n_here, n_there = here_ref.shape[0], there_ref.shape[0]

    def load(s):
        return pltpu.make_async_copy(got_hbm.at[s], got_ref.at[s], sems.at[s])

    @pl.loop(0, got_ref.shape[0])
    def _(s):
        @pl.when(labels_ref[s] >= 0)
        def _():
            load(s).start()

    @pl.loop(0, n_here)
    def _(t):
        here_ref[t] = jnp.zeros(here_ref.shape[1:], jnp.float32)

    @pl.loop(0, n_there)
    def _(t):
        sum_ref[t] = jnp.zeros(sum_ref.shape[1:], jnp.float32)

    @pl.loop(0, got_ref.shape[0])
    def _(s):
        label = labels_ref[s]

        @pl.when(label >= 0)
        def _():
            load(s).wait()

        @pl.when((label >= 0) & (label < n_here))
        def _():
            here_ref[label] += got_ref[s].astype(jnp.float32)

        @pl.when(label >= n_here)
        def _():
            sum_ref[label - n_here] += got_ref[s].astype(jnp.float32)

    @pl.loop(0, n_there)
    def _(t):
        there_ref[t] = sum_ref[t].astype(there_ref.dtype)


def table_of(labels, got, n_here, n_there):
    vmem = pl.BlockSpec(memory_space=pltpu.VMEM)
    return pl.pallas_call(
        table_kernel,
        out_shape=[
            jax.ShapeDtypeStruct((n_here, W, W), jnp.float32),
            jax.ShapeDtypeStruct((n_there, W, W), jnp.bfloat16),
        ],
        in_specs=[pl.BlockSpec(memory_space=pltpu.SMEM), pl.BlockSpec(memory_space=pltpu.HBM)],
        out_specs=[vmem] * 2,
        scratch_shapes=[
            pltpu.VMEM(got.shape, got.dtype),
            pltpu.VMEM((n_there, W, W), jnp.float32),
            pltpu.SemaphoreType.DMA((got.shape[0],)),
        ],
        compiler_params=pltpu.CompilerParams(vmem_limit_bytes=24 << 20),
        cost_estimate=pl.CostEstimate(flops=2_000_000, bytes_accessed=7_000_000, transcendentals=0),
        name="table_of",
    )(labels, got)


def sum_over_groups(labels, got):
    groups, cores = lax.axis_size("grp"), 2
    n_y = groups // cores
    y, core = lax.axis_index("grp") // cores, lax.axis_index("grp") % cores
    to, place = labels // CT, labels % CT
    dy = (to // cores - y) % n_y
    other = (to % cores - core) % cores
    at = jnp.where(labels < 0, -1, (other * n_y + dy) * CT + place)
    here, there = table_of(at, got, n_y * CT, n_y * CT)
    swap = [(g, g // cores * cores + (g + 1) % cores) for g in range(groups)]
    here += lax.ppermute(there, "grp", swap).astype(jnp.float32)
    total = here[:CT]
    for step in (2, 1, 3):
        pairs = [(g, (g + step * cores) % groups) for g in range(groups)]
        part = here[step * CT : (step + 1) * CT].astype(jnp.bfloat16)
        total += lax.ppermute(part, "grp", pairs).astype(jnp.float32)
    return total


def layer(blocks, prolong, block_cols, fetch_rows, tile_slot, tile_owner, tile_place):
    dev_count = lax.axis_size("dev")
    panels = prolong[0, 0]
    owners = tile_owner[0, 0]
    dev_target = owners % dev_count
    label = (owners // dev_count) * CT + tile_place[0, 0]
    meant = dev_target[None, :] == jnp.arange(dev_count)[:, None]
    labels = jnp.max(jnp.where(meant, label[None, :], -1), axis=1)
    pieces, spots, where, got_labels = fetch(panels, fetch_rows[0, 0], labels)

    pt = panels.reshape(R * BLOCK, W).T
    sending = device_tiles(
        blocks[0, 0], pt, pieces, spots, where, block_cols[0, 0], tile_slot[0, 0], dev_target, dev_count
    )
    got = lax.all_to_all(sending, "dev", split_axis=0, concat_axis=0, tiled=True)
    return sum_over_groups(got_labels, got).reshape(1, 1, CT, W, W)


def solution(mesh):
    return jax.shard_map(
        layer,
        mesh=mesh,
        in_specs=(
            P("grp", "dev", None, None, None),
            P("grp", "dev", None, None, None),
            P("grp", "dev", None, None),
            P("grp", "dev", None, None),
            P("grp", "dev", None, None),
            P("grp", "dev", None),
            P("grp", "dev", None),
        ),
        out_specs=P("grp", "dev", None, None, None),
        check_vma=False,
    )
```
